256 devices in a mesh: depth: 128 (over x, y, z), slab: 2 (over core).
Axes of the slice: x: 4, y: 4, z: 8, core: 2. Of those that a mesh axis runs over, the one named last changes fastest.
Arguments:
- ref_feat: bfloat16 [4, 32, 128], P('slab'), may hold values from -9 to 9
- src_feat: bfloat16 [20480, 32, 128], P('depth'), may hold values from -9 to 9
- tile_owner: int32 [10240, 1], P(('depth', 'slab')), may hold values from 0 to 127; in each aligned block of 40 rows (0 to 39, 40 to 79, ...) at most 2 rows name the same one
- tile_local: int32 [10240], P(('depth', 'slab')), may hold values from 0 to 159
- col_shift: int32 [10240], P(('depth', 'slab')), may hold values from -16 to 16
- w_gates: bfloat16 [9, 64, 8], replicated, may hold values from -1.4375 to 1.4375
- bias_z: float32 [32], replicated
- bias_c: float32 [32], replicated, may hold values from -3 to 3
- w_out: float32 [32], replicated
Outputs:
- probability: float32 [512, 4, 128], P('depth', 'slab')
- depth_map: float32 [4, 128], P('slab')
The draws below stay inside these ranges and needn't reach their ends.
Inputs may be any that keep to these rules, and one draw needn't show every extreme that they name: `tile_owner`: among the requests of one device no owner is named more than 2 times; in some devices one owner is named exactly 2 times.
All inputs are finite; a program needn't handle non-finite values.
Results may differ from the reference program's by a relative error of at most 0.00085.
Values may be sent and summed in bfloat16 or wider, within the bound.
No kernel may reach another device: no remote copies, remote signals or barrier semaphores. Data moves between devices by JAX's collectives and lax.ppermute only.
A program may use at most 64 MiB of HBM per device.

```python
import math
import jax
import jax.numpy as jnp
import numpy as np
from jax import lax

FEAT = 32
GROUPS = 8
HID = 32
VIEWS = 5
PD = 4
COLS = 128
MAXSHIFT = 16
RS = 2
SRC_DEV = 160
PLANES = 512
ROWS = 4
CPG = 4
REQ_DEV = 40
REQUESTS = 10240
CAP = 2
SRC_TILES = 20480
N_DEPTH = 128
N_SLAB = 2


def draw_bias_z(key, part):
    key_kind, key_slow, key_fast = jax.random.split(key, 3)
    kind_draw = jax.random.randint(key_kind, (HID,), 0, 2)
    slow_units = kind_draw < 1
    keep_rate = jax.random.uniform(key_slow, (HID,), jnp.float32, 0.3, 1.2)
    span_top = jnp.log(jnp.float32(max(PLANES / 4.0, 4.0)))
    span_log = jax.random.uniform(key_fast, (HID,), jnp.float32, 0.0, 1.0)
    fast_span = jnp.exp(jnp.log(jnp.float32(2.0)) + span_log * (span_top - jnp.log(jnp.float32(2.0))))
    log_retain = jnp.where(slow_units, -keep_rate / PLANES, -1.0 / fast_span)
    return (log_retain - jnp.log(-jnp.expm1(log_retain))).astype(jnp.float32)


def draw_w_out(key, part):
    return (jax.random.normal(key, (HID,), jnp.float32) * 3.0).astype(jnp.float32)


def set_ends(entries, rng, least, high):
    place = [jax.random.randint(jax.random.fold_in(rng, axis), (), 0, length) for axis, length in enumerate(entries.shape)]
    main_axis = entries.shape.index(max(entries.shape))
    neighbour = place[:main_axis] + [(place[main_axis] + 1) % entries.shape[main_axis]] + place[main_axis + 1:]
    return entries.at[tuple(place)].set(least).at[tuple(neighbour)].set(high)


def block_levels(own_key, extent, pieces, low, high):
    def one(dim, blocks):
        draws = jax.random.uniform(jax.random.fold_in(jax.random.fold_in(own_key, 6), dim), (blocks,), jnp.float32, low / len(pieces), high / len(pieces))
        return jnp.repeat(jnp.exp(draws), extent[dim] // blocks).reshape((-1,) + (1,) * (len(extent) - dim - 1))

    factor_of = one(*pieces[0])
    for cut in pieces[1:]:
        factor_of = factor_of * one(*cut)
    return factor_of


def shared_out(rng, own, number, rows, amount, top, reach, slope):
    order = jax.random.permutation(rng, amount)
    heavy_load, usual = load_shares(amount, rows * top, reach, slope, True), load_shares(amount, rows * top, reach, slope, False)
    places = jnp.arange(amount)

    def named(tallies, offset_by):
        used = int((tallies > 0).sum())
        fixed = max(1, used // 4)
        moved = fixed + (places - fixed + offset_by * (used - fixed)) % max(1, amount - fixed)
        return jnp.zeros((amount,), jnp.int32).at[order[jnp.where(places < fixed, places, moved)]].set(jnp.asarray(tallies, jnp.int32))

    tallies = jnp.where(number % 4 == 0, named(heavy_load, number // 4), named(usual, number - number // 4 - 1))
    mixed = jax.random.permutation(jax.random.fold_in(own, 3), amount)
    source_of, receiver = mixed[0:amount // 2 * 2:2], mixed[1:amount // 2 * 2:2]
    room = jnp.minimum(tallies[source_of] - 1, reach - tallies[receiver]) // 2
    room = jnp.where((source_of == order[0]) | (receiver == order[0]) | (tallies[receiver] == 0), 0, jnp.maximum(room, 0))
    moved = jax.random.randint(jax.random.fold_in(own, 4), (amount // 2,), 0, 1 << 20) % (room + 1)
    tallies = tallies.at[source_of].add(-moved).at[receiver].add(moved)
    members = jnp.searchsorted(jnp.cumsum(tallies), jnp.arange(rows * top), side="right").astype(jnp.int32)
    table = members.reshape(top, rows).T
    table = table[jax.random.permutation(jax.random.fold_in(own, 1), rows)]
    offset_by = jax.random.randint(jax.random.fold_in(own, 2), (rows, 1), 0, top)
    return jnp.take_along_axis(table, (jnp.arange(top)[None, :] + offset_by) % top, axis=1)


def load_shares(amount, total, bound, skew, full):
    weights = [(1 << 20) // math.isqrt(grade ** skew) + 1 for grade in range(1, amount + 1)]
    largest = bound if full else min(bound, max(-(-total // amount), total * weights[0] // sum(weights)))
    least = 1 if total - largest >= amount - 1 else 0
    given, spare = [largest] + [least] * (amount - 1), total - largest - least * (amount - 1)
    while spare > 0:
        movable = [i for i in range(1, amount) if given[i] < largest] or [i for i in range(1, amount) if given[i] < bound]
        whole, budget = sum([weights[i] for i in movable]), spare
        for i in movable:
            addition = min(bound - given[i], max(1, budget * weights[i] // whole), spare)
            given[i] = given[i] + addition
            spare = spare - addition
    return np.array(given)


def centred(rng, dims, spread, reach, shards=(), kind=jnp.bfloat16):
    result = jax.random.normal(rng, dims, jnp.float32) * spread
    if len(shards) > 0:
        result = block_levels(rng, dims, shards, -0.22, 0.18) * result
    return jnp.clip(result, min=-reach, max=reach).astype(kind)


def setup_inputs(seed: int = 0) -> dict:
    splits = jax.random.split(jax.random.key(seed), 10)
    ref_feat = centred(splits[0], (ROWS, FEAT, COLS), 1.5, 9.0, ((0, 2),))
    src_feat = centred(splits[1], (SRC_TILES, FEAT, COLS), 1.5, 9.0, ((0, 128),))
    tile_owner_keys = jax.random.split(jax.random.fold_in(splits[2], 1), REQUESTS // REQ_DEV)
    tile_owner_turns = jax.random.permutation(jax.random.fold_in(splits[2], 3), REQUESTS // REQ_DEV)
    tile_owner = jax.vmap(lambda own, number: shared_out(jax.random.fold_in(splits[2], 2), own, number, REQ_DEV, N_DEPTH, 1, CAP, 2))(tile_owner_keys, tile_owner_turns).reshape((REQUESTS, 1))
    tile_local = set_ends(jax.random.randint(splits[3], (REQUESTS,), 0, SRC_DEV), jax.random.fold_in(splits[3], 1), 0, SRC_DEV - 1).astype(jnp.int32)
    col_shift = set_ends(jax.random.randint(splits[4], (REQUESTS,), 0 - MAXSHIFT, MAXSHIFT + 1), jax.random.fold_in(splits[4], 1), 0 - MAXSHIFT, MAXSHIFT).astype(jnp.int32)
    w_gates = centred(splits[5], (9, 2 * HID, GROUPS), 0.24, 1.4375)
    bias_z = draw_bias_z(jax.random.fold_in(splits[9], 71), 0)
    bias_c = centred(splits[7], (HID,), 0.5, 3.0, (), jnp.float32)
    w_out = draw_w_out(jax.random.fold_in(splits[9], 71), 0)
    return {"ref_feat": ref_feat, "src_feat": src_feat, "tile_owner": tile_owner, "tile_local": tile_local, "col_shift": col_shift, "w_gates": w_gates, "bias_z": bias_z, "bias_c": bias_c, "w_out": w_out}


def arrange(values):
    shaped = values.reshape(N_DEPTH, N_SLAB, PD, VIEWS, RS)
    return shaped.transpose(0, 2, 3, 1, 4).reshape(PLANES, VIEWS, ROWS)


def reference(ref_feat, src_feat, tile_owner, tile_local, col_shift, w_gates, bias_z, bias_c, w_out):
    tile_all = arrange(tile_owner[:, 0].astype(jnp.int32) * SRC_DEV + tile_local.astype(jnp.int32))
    shift_all = arrange(col_shift.astype(jnp.int32))
    ref_wide = ref_feat.astype(jnp.float32)
    positions = jnp.arange(COLS, dtype=jnp.int32)
    gates_wide = w_gates.astype(jnp.float32)

    def plane_step(current, inputs):
        tile_ids, shift_now = inputs
        tile_rows = jnp.take(src_feat, tile_ids.reshape(-1), axis=0).reshape(VIEWS, ROWS, FEAT, COLS)
        source_col = positions[None, None, :] - shift_now[:, :, None]
        inside = (source_col >= 0) & (source_col < COLS)
        clipped = jnp.clip(source_col, 0, COLS - 1)
        index_full = jnp.broadcast_to(clipped[:, :, None, :], tile_rows.shape)
        moved = jnp.take_along_axis(tile_rows, index_full, axis=3)
        warped = jnp.where(inside[:, :, None, :], moved, jnp.zeros((), tile_rows.dtype))
        product = warped.astype(jnp.float32) * ref_wide[None]
        summed = product.reshape(VIEWS, ROWS, GROUPS, CPG, COLS).sum(axis=(0, 3))
        cost = summed / (VIEWS * CPG)
        padded = jnp.pad(cost, ((1, 1), (0, 0), (1, 1)))
        preact = jnp.zeros((ROWS, 2 * HID, COLS), jnp.float32)
        for tap_index in range(9):
            row_step = tap_index // 3
            col_step = tap_index % 3
            window = padded[row_step:row_step + ROWS, :, col_step:col_step + COLS]
            preact = preact + jnp.einsum("rgx,og->rox", window, gates_wide[tap_index], precision=lax.Precision.HIGHEST)
        retain = jax.nn.sigmoid(preact[:, :HID] + bias_z[None, :, None])
        candidate = jnp.tanh(preact[:, HID:] + bias_c[None, :, None])
        current = retain * current + (1.0 - retain) * candidate
        score = jnp.einsum("rox,o->rx", current, w_out, precision=lax.Precision.HIGHEST)
        return current, score

    start = jnp.zeros((ROWS, HID, COLS), jnp.float32)
    final_state, scores = lax.scan(plane_step, start, (tile_all, shift_all))
    highest = jnp.max(scores, axis=0)
    weights = jnp.exp(scores - highest[None])
    totals = jnp.sum(weights, axis=0)
    probability = weights / totals[None]
    plane_index = jnp.arange(PLANES, dtype=jnp.int32).astype(jnp.float32)
    depth_value = 1.0 / (0.1 + 0.9 * plane_index / (PLANES - 1))
    depth_map = jnp.sum(probability * depth_value[:, None, None], axis=0)
    return probability, depth_map
```

```python
import jax
import jax.numpy as jnp
from jax import lax
from jax.experimental import pallas as pl
from jax.experimental.pallas import tpu as pltpu
from jax.sharding import PartitionSpec as P

VIEWS = 5
PD = 4
MAXSHIFT = 16
F32 = jnp.float32
BF16 = jnp.bfloat16
VMEM_LIMIT = 40 * 1024 * 1024


def params():
    return pltpu.CompilerParams(vmem_limit_bytes=VMEM_LIMIT)


def vspec():
    return pl.BlockSpec(memory_space=pltpu.VMEM)


def sspec():
    return pl.BlockSpec(memory_space=pltpu.SMEM)


def prepare_kernel(ref_ref, src_ref, tab_ref, srce_ref, ref32, src32):
    rows, feat, cols = ref_ref.shape
    tiles = src_ref.shape[0]
    cpg = feat // 8
    for r in range(rows):
        ref32[pl.ds(r * feat, feat), :] = ref_ref[r].astype(F32)
    lane = lax.broadcasted_iota(jnp.int32, (8, cols), 1)
    for r in range(rows):
        for e in range(cpg):
            base = ref32[pl.ds(r * feat + e, 8, stride=cpg), :]
            for k in range(2 * MAXSHIFT + 1):
                shift = k - MAXSHIFT
                moved = base if shift == 0 else pltpu.roll(base, (-shift) % cols, 1)
                inside = (lane + shift >= 0) & (lane + shift < cols)
                tab_ref[r * (2 * MAXSHIFT + 1) + k, pl.ds(e * 8, 8), :] = jnp.where(inside, moved, 0.0)

    def widen(n, c):
        src32[pl.ds(n * feat, feat), :] = src_ref[n].astype(F32)
        return c

    lax.fori_loop(0, tiles, widen, 0, unroll=8)

    def reorder(n, c):
        parts = [src32[pl.ds(n * feat + e, 8, stride=cpg), :] for e in range(cpg)]
        srce_ref[n] = jnp.concatenate(parts, axis=0).astype(BF16)
        return c

    lax.fori_loop(0, tiles, reorder, 0, unroll=8)


def answer_kernel(requests, req_ref, tab_ref, srce_ref, out_ref, codes, table, sem):
    owners = req_ref.shape[0]
    cols = out_ref.shape[-1]
    me = lax.axis_index("depth")
    flat = req_ref[...].T
    owner = flat[0:requests]
    local = flat[requests : 2 * requests]
    shift = flat[2 * requests : 3 * requests]
    q = lax.broadcasted_iota(jnp.int32, (requests, owners), 0)
    hit = owner == me
    first = jnp.min(jnp.where(hit, q, requests), axis=0, keepdims=True)
    last = jnp.max(jnp.where(hit, q, -1), axis=0, keepdims=True)
    value = local + (shift + MAXSHIFT) * 256 + (q % 2) * 16384
    zero = jnp.zeros_like(value)
    code0 = jnp.sum(jnp.where(hit & (q == first), value, zero), axis=0, keepdims=True)
    code1 = jnp.sum(jnp.where(hit & (q == last) & (q > first), value, zero), axis=0, keepdims=True)
    sub = lax.broadcasted_iota(jnp.int32, (8, owners), 0)
    codes[...] = jnp.where(sub == 0, code0, jnp.where(sub == 1, code1, 0))
    copy = pltpu.make_async_copy(codes, table, sem)
    copy.start()
    copy.wait()

    def one(i, s):
        code = table[s, i]
        loc = code & 255
        moved = (code >> 8) & 63
        row = code >> 14
        tile = srce_ref[loc].astype(F32) * tab_ref[row * (2 * MAXSHIFT + 1) + moved]
        total = (tile[0:8] + tile[8:16]) + (tile[16:24] + tile[24:32])
        out_ref[i * 2 + s] = pltpu.roll(total, (moved + cols - MAXSHIFT) % cols, 1)

    def step(i, c):
        one(i, 0)
        one(i, 1)
        return c

    lax.fori_loop(0, owners, step, 0, unroll=8)


def cost_kernel(idx_ref, ans_ref, out_ref):
    cols = ans_ref.shape[-1]
    lane = lax.broadcasted_iota(jnp.int32, (8, cols), 1)
    for h in range(2):
        rows = []
        for pp in range(2):
            for r in range(2):
                acc = None
                for v in range(VIEWS):
                    part = ans_ref[idx_ref[(2 * h + pp) * 2 * VIEWS + v * 2 + r]]
                    acc = part if acc is None else acc + part
                c = acc / (VIEWS * 4.0)
                rows.append(jnp.where(lane == 0, 0.0, pltpu.roll(c, 1, 1)))
                rows.append(c)
                rows.append(jnp.where(lane == cols - 1, 0.0, pltpu.roll(c, cols - 1, 1)))
        rows.append(jnp.zeros((32, cols), F32))
        block = jnp.concatenate(rows, axis=0).T
        out_ref[pl.ds(h, cols, stride=4), :] = block
        out_ref[pl.ds(2 + h, cols, stride=4), :] = block


def column_kernel(x_ref, w_ref, bias_ref, wo_ref, out_ref, d_s, o_s, hb_s, dp_s, op_s):
    n = x_ref.shape[0] // 4
    tops = []
    for h in range(2):
        tops.append(
            jnp.concatenate(
                [x_ref[pl.ds(h, n, stride=4), :], x_ref[pl.ds(2 + h, n, stride=4), :]], axis=1
            )
        )
    x = jnp.concatenate(tops, axis=0)
    w = w_ref[...]
    hi = x.astype(BF16)
    rest = x - hi.astype(F32)
    mid = rest.astype(BF16)
    low = (rest - mid.astype(F32)).astype(BF16)
    y = jnp.dot(low, w, preferred_element_type=F32)
    y = y + jnp.dot(mid, w, preferred_element_type=F32)
    y = y + jnp.dot(hi, w, preferred_element_type=F32)
    z = y[:, :128] + bias_ref[0:1, :]
    cand = jnp.tanh(y[:, 128:] + bias_ref[1:2, :])
    small = jnp.exp(-jnp.abs(z))
    big = 1.0 / (1.0 + small)
    small = small * big
    up = z >= 0
    retain = jnp.where(up, big, small)
    fresh = jnp.where(up, small, big) * cand
    lane = lax.broadcasted_iota(jnp.int32, (2 * n, 128), 1)
    low_half = lane < 64
    other_r = pltpu.roll(retain, 64, 1)
    other_f = pltpu.roll(fresh, 64, 1)
    pair_d = retain * other_r
    pair_o = jnp.where(low_half, other_r * fresh + other_f, retain * other_f + fresh)
    d_s[...] = pair_d
    o_s[...] = pair_o
    per = n // 8
    dc = jnp.ones((8, 128), F32)
    oc = jnp.zeros((8, 128), F32)
    for ii in range(per):
        for h in range(2):
            step = ii * 2 + h
            d = d_s[pl.ds(h * n + ii, 8, stride=per), :]
            o = o_s[pl.ds(h * n + ii, 8, stride=per), :]
            dp_s[step] = dc
            op_s[step] = oc
            oc = d * oc + o
            dc = d * dc
    sub = lax.broadcasted_iota(jnp.int32, (8, 128), 0)
    start = jnp.zeros((8, 128), F32)
    for _ in range(7):
        start = jnp.where(sub == 0, 0.0, pltpu.roll(dc * start + oc, 1, 0))
    for ii in range(per):
        for h in range(2):
            step = ii * 2 + h
            hb_s[pl.ds(h * n + ii, 8, stride=per), :] = dp_s[step] * start + op_s[step]
    hb = hb_s[...]
    state = jnp.where(low_half, retain, pair_d) * hb + jnp.where(low_half, fresh, pair_o)
    wide = jnp.concatenate([state[:n], state[n:]], axis=1)
    s = jnp.dot(wide, wo_ref[...], precision=lax.Precision.HIGHEST, preferred_element_type=F32)

    def over(op, v):
        v = jnp.broadcast_to(v, (8, 128))
        v = op(v, pltpu.roll(v, 2, 1))
        return op(v, pltpu.roll(v, 4, 1))[0:1]

    row = lax.broadcasted_iota(jnp.int32, (n, 128), 0)
    col = lax.broadcasted_iota(jnp.int32, (n, 128), 1)
    plane = row * PD + (col % 8) // 2
    value = 1.0 / (0.1 + 0.9 * plane.astype(F32) / (PD * n - 1))
    highest = over(jnp.maximum, jnp.max(s, axis=0, keepdims=True))
    weights = jnp.exp(s - highest)
    total = over(jnp.add, jnp.sum(weights, axis=0, keepdims=True))
    depth = over(jnp.add, jnp.sum(weights * value, axis=0, keepdims=True))
    out_ref[...] = jnp.where(col < 8, weights / total, depth / total)


def output_kernel(x_ref, prob_ref, map_ref):
    t = x_ref[...].T
    for p in range(PD):
        prob_ref[p] = t[p * 2 : p * 2 + 2]
    map_ref[...] = t[8:10]


def gate_matrix(w_gates, slab):
    w = w_gates.reshape(3, 3, 2, 32, 8).transpose(0, 1, 4, 2, 3)
    w = jnp.pad(w, ((2, 2), (0, 0), (0, 0), (0, 0), (0, 0)))
    by_row = [
        lax.dynamic_slice_in_dim(w, 3 - r - 2 * slab, 4, axis=0) for r in range(2)
    ]
    v = jnp.stack(by_row, axis=4).reshape(2, 2, 3, 8, 2, 2, 32)
    same = jnp.eye(2, dtype=w.dtype)
    full = v[:, None, :, :, :, :, None] * same[None, :, None, None, None, None, :, None, None]
    full = full.reshape(2, 96, 256)
    return jnp.pad(full, ((0, 0), (0, 32), (0, 0))).reshape(256, 256)


def body(ref_feat, src_feat, tile_owner, tile_local, col_shift, w_gates, bias_z, bias_c, w_out):
    owners = lax.axis_size("depth")
    row_count, feat, cols = ref_feat.shape
    requests = tile_local.shape[0]
    tiles = src_feat.shape[0]
    owner = tile_owner[:, 0]
    message = jnp.concatenate(
        [owner, tile_local, col_shift, jnp.zeros((128 - 3 * requests,), jnp.int32)]
    )
    message = jnp.broadcast_to(message[None, None, :], (owners, 1, 128))
    asked = lax.all_to_all(message, "depth", split_axis=0, concat_axis=0, tiled=True)

    table, channels = pl.pallas_call(
        prepare_kernel,
        out_shape=(
            jax.ShapeDtypeStruct((row_count * (2 * MAXSHIFT + 1), feat, cols), F32),
            jax.ShapeDtypeStruct((tiles, feat, cols), BF16),
        ),
        in_specs=[vspec(), vspec()],
        out_specs=(vspec(), vspec()),
        scratch_shapes=[
            pltpu.VMEM((row_count * feat, cols), F32),
            pltpu.VMEM((tiles * feat, cols), F32),
        ],
        compiler_params=params(),
        cost_estimate=pl.CostEstimate(flops=2000000, transcendentals=0, bytes_accessed=4000000),
        name="prepare",
    )(ref_feat, src_feat)

    def answers_of(*refs):
        answer_kernel(requests, *refs)

    answers = pl.pallas_call(
        answers_of,
        out_shape=jax.ShapeDtypeStruct((owners * 2, 8, cols), F32),
        in_specs=[vspec(), vspec(), vspec()],
        out_specs=vspec(),
        scratch_shapes=[
            pltpu.VMEM((8, owners), jnp.int32),
            pltpu.SMEM((8, owners), jnp.int32),
            pltpu.SemaphoreType.DMA,
        ],
        compiler_params=params(),
        name="answer",
    )(asked.reshape(owners, 128), table, channels)
    answers = lax.all_to_all(
        answers.reshape(owners, 16, cols), "depth", split_axis=0, concat_axis=0, tiled=True
    )

    q = jnp.arange(requests, dtype=jnp.int32)
    earlier = (owner[:, None] == owner[None, :]) & (q[None, :] < q[:, None])
    index = owner * 2 + jnp.any(earlier, axis=1).astype(jnp.int32)
    costs = pl.pallas_call(
        cost_kernel,
        out_shape=jax.ShapeDtypeStruct((cols * 4, 128), F32),
        in_specs=[sspec(), vspec()],
        out_specs=vspec(),
        compiler_params=params(),
        name="cost",
    )(index, answers.reshape(owners * 2, 8, cols))
    costs = lax.all_to_all(
        costs.reshape(cols * 2, 2, 128), ("depth", "slab"), split_axis=0, concat_axis=0, tiled=True
    )

    slab = lax.axis_index("slab")
    gates = gate_matrix(w_gates, slab)
    bias = jnp.stack([jnp.tile(bias_z, 4), jnp.tile(bias_c, 4)])
    unit_row = jnp.arange(256, dtype=jnp.int32)[:, None] // 32
    score_col = jnp.arange(128, dtype=jnp.int32)[None, :] % 8
    project = jnp.where(unit_row == score_col, jnp.tile(w_out, 8)[:, None], 0.0)
    packed = pl.pallas_call(
        column_kernel,
        out_shape=jax.ShapeDtypeStruct((owners, 128), F32),
        in_specs=[vspec()] * 4,
        out_specs=vspec(),
        scratch_shapes=[
            pltpu.VMEM((2 * owners, 128), F32),
            pltpu.VMEM((2 * owners, 128), F32),
            pltpu.VMEM((2 * owners, 128), F32),
            pltpu.VMEM((owners // 4, 8, 128), F32),
            pltpu.VMEM((owners // 4, 8, 128), F32),
        ],
        compiler_params=params(),
        name="column",
    )(costs.reshape(cols * 4, 128), gates, bias, project)
    packed = lax.all_to_all(
        packed.reshape(owners, 1, 128), "depth", split_axis=0, concat_axis=0, tiled=True
    )
    return pl.pallas_call(
        output_kernel,
        out_shape=(
            jax.ShapeDtypeStruct((PD, row_count, cols), F32),
            jax.ShapeDtypeStruct((row_count, cols), F32),
        ),
        in_specs=[vspec()],
        out_specs=(vspec(), vspec()),
        compiler_params=params(),
        name="output",
    )(packed.reshape(cols, 128))


def solution(mesh):
    return jax.shard_map(
        body,
        mesh=mesh,
        in_specs=(
            P("slab", None, None),
            P("depth", None, None),
            P(("depth", "slab"), None),
            P(("depth", "slab")),
            P(("depth", "slab")),
            P(),
            P(),
            P(),
            P(),
        ),
        out_specs=(P("depth", "slab", None), P("slab", None)),
        check_vma=False,
    )
```

```python
import jax
import jax.numpy as jnp
from jax import lax
from jax.experimental import pallas as pl
from jax.experimental.pallas import tpu as pltpu
from jax.sharding import PartitionSpec as P

VIEWS = 5
PD = 4
MAXSHIFT = 16
F32 = jnp.float32
BF16 = jnp.bfloat16
VMEM_LIMIT = 40 * 1024 * 1024


def params():
    return pltpu.CompilerParams(vmem_limit_bytes=VMEM_LIMIT)


def vspec():
    return pl.BlockSpec(memory_space=pltpu.VMEM)


def sspec():
    return pl.BlockSpec(memory_space=pltpu.SMEM)


def prepare_kernel(ref_ref, src_ref, tab_ref, srce_ref, ref32, src32):
    rows, feat, cols = ref_ref.shape
    tiles = src_ref.shape[0]
    cpg = feat // 8
    for r in range(rows):
        ref32[pl.ds(r * feat, feat), :] = ref_ref[r].astype(F32)
    lane = lax.broadcasted_iota(jnp.int32, (8, cols), 1)
    for r in range(rows):
        for e in range(cpg):
            base = ref32[pl.ds(r * feat + e, 8, stride=cpg), :]
            for k in range(2 * MAXSHIFT + 1):
                shift = k - MAXSHIFT
                moved = base if shift == 0 else pltpu.roll(base, (-shift) % cols, 1)
                inside = (lane + shift >= 0) & (lane + shift < cols)
                tab_ref[r * (2 * MAXSHIFT + 1) + k, pl.ds(e * 8, 8), :] = jnp.where(inside, moved, 0.0)

    def widen(n, c):
        src32[pl.ds(n * feat, feat), :] = src_ref[n].astype(F32)
        return c

    lax.fori_loop(0, tiles, widen, 0, unroll=8)

    def reorder(n, c):
        parts = [src32[pl.ds(n * feat + e, 8, stride=cpg), :] for e in range(cpg)]
        srce_ref[n] = jnp.concatenate(parts, axis=0).astype(BF16)
        return c

    lax.fori_loop(0, tiles, reorder, 0, unroll=8)


def answer_kernel(requests, req_ref, tab_ref, srce_ref, out_ref, codes, table, sem):
    owners = req_ref.shape[0]
    cols = out_ref.shape[-1]
    me = lax.axis_index("depth")
    flat = req_ref[...].T
    owner = flat[0:requests]
    local = flat[requests : 2 * requests]
    shift = flat[2 * requests : 3 * requests]
    q = lax.broadcasted_iota(jnp.int32, (requests, owners), 0)
    hit = owner == me
    first = jnp.min(jnp.where(hit, q, requests), axis=0, keepdims=True)
    last = jnp.max(jnp.where(hit, q, -1), axis=0, keepdims=True)
    value = local + (shift + MAXSHIFT) * 256 + (q % 2) * 16384
    zero = jnp.zeros_like(value)
    code0 = jnp.sum(jnp.where(hit & (q == first), value, zero), axis=0, keepdims=True)
    code1 = jnp.sum(jnp.where(hit & (q == last) & (q > first), value, zero), axis=0, keepdims=True)
    sub = lax.broadcasted_iota(jnp.int32, (8, owners), 0)
    codes[...] = jnp.where(sub == 0, code0, jnp.where(sub == 1, code1, 0))
    copy = pltpu.make_async_copy(codes, table, sem)
    copy.start()
    copy.wait()

    def one(i, s):
        code = table[s, i]
        loc = code & 255
        moved = (code >> 8) & 63
        row = code >> 14
        tile = srce_ref[loc].astype(F32) * tab_ref[row * (2 * MAXSHIFT + 1) + moved]
        total = (tile[0:8] + tile[8:16]) + (tile[16:24] + tile[24:32])
        return pltpu.roll(total, (moved + cols - MAXSHIFT) % cols, 1)

    def step(b, c):
        parts = []
        for il in range(8):
            for s in range(2):
                parts.append(one(b * 8 + il, s))
        block = jnp.concatenate(parts, axis=0).T
        out_ref[pl.ds(b, cols, stride=owners // 8), :] = block
        return c

    lax.fori_loop(0, owners // 8, step, 0, unroll=2)


def table_kernel(requests, req_ref, wd_ref, target_ref, gate_ref, keys):
    owners = req_ref.shape[0]
    blocks = owners // 8
    flat = req_ref[...].T
    owner = flat[0:requests]
    q = lax.broadcasted_iota(jnp.int32, (requests, owners), 0)
    earlier = jnp.zeros((requests, owners), jnp.int32)
    for other in range(requests - 1):
        same = (owner == owner[other : other + 1]) & (q > other)
        earlier = jnp.where(same, 1, earlier)
    key = (owner * 2 + earlier).astype(F32)
    block_row = lax.broadcasted_iota(jnp.int32, (blocks, owners), 0)
    block_of = lax.broadcasted_iota(jnp.int32, (blocks, owners), 1) // 8
    own_block = block_row == block_of
    spread = []
    for n in range(requests):
        row = jnp.broadcast_to(key[n : n + 1], (blocks, owners))
        spread.append(jnp.where(own_block, row, 0.0).astype(BF16))
    inner = lax.broadcasted_iota(jnp.int32, (owners, 128), 0) % 8
    lane = lax.broadcasted_iota(jnp.int32, (owners, 128), 1)
    pick = jnp.where(inner == lane // 16, 1.0, 0.0).astype(BF16)
    wide = jnp.dot(jnp.concatenate(spread, axis=0), pick, preferred_element_type=F32)
    slot = (lax.broadcasted_iota(jnp.int32, (blocks * requests, 128), 1) // 8) % 2
    keys[...] = wide - slot.astype(F32)

    def step(n, c):
        found = [[jnp.full((8, 128), 8.0, F32) for _ in range(blocks // 8)] for _ in range(4)]
        wanted = [(2 * (n * 4 + m)).astype(F32) for m in range(4)]
        for r in range(requests):
            t = float((r // (2 * VIEWS)) * 2 + r % 2)
            for half in range(blocks // 8):
                k = keys[r * blocks + half * 8 : r * blocks + half * 8 + 8, :]
                for m in range(4):
                    found[m][half] = jnp.where(k == wanted[m], t, found[m][half])
        for m in range(4):
            for half in range(blocks // 8):
                target_ref[n * 4 + m, half * 8 : half * 8 + 8, :] = found[m][half]
        return c

    lax.fori_loop(0, owners // 4, step, 0)

    half_of = lax.broadcasted_iota(jnp.int32, (16, 128), 1) // 64
    for source in range(6):
        for zc in range(2):
            part = wd_ref[zc, source * 16 : source * 16 + 16, :]
            for il in range(8):
                mine = jnp.where(half_of == il // 4, part, jnp.zeros_like(part))
                for il3 in range(4):
                    value = mine if il3 == il % 4 else jnp.zeros_like(part)
                    gate_ref[
                        pl.ds(source * 128 + il * 16, 16), pl.ds((zc * 4 + il3) * 128, 128)
                    ] = value


def combine_kernel(ans_ref, target_ref, out_ref):
    owners = ans_ref.shape[0]
    halves = ans_ref.shape[1] // 8

    def step(o, acc):
        acc = list(acc)
        for half in range(halves):
            data = ans_ref[o, half * 8 : half * 8 + 8, :]
            target = target_ref[o, half * 8 : half * 8 + 8, :]
            for t in range(8):
                n = t * halves + half
                acc[n] = acc[n] + jnp.where(target == float(t), data, 0.0)
        return tuple(acc)

    zero = jnp.zeros((8, 128), F32)
    acc = lax.fori_loop(0, owners, step, (zero,) * (8 * halves), unroll=8)
    lane = lax.broadcasted_iota(jnp.int32, (8, 128), 1)
    even = (lane // 8) % 2 == 0
    for p in range(PD):
        for half in range(halves):
            a = acc[(2 * p) * halves + half]
            b = acc[(2 * p + 1) * halves + half]
            a = a + pltpu.roll(a, 120, 1)
            b = b + pltpu.roll(b, 8, 1)
            out_ref[pl.ds((p * halves + half) * 8, 8), :] = jnp.where(even, a, b) / (VIEWS * 4.0)


def column_kernel(left_ref, mid_ref, right_ref, w_ref, bias_ref, wo_ref, out_ref):
    rows = mid_ref.shape[0] // 2
    blocks = rows // PD
    x = jnp.concatenate(
        [ref[pl.ds(j * rows, rows), :] for ref in (left_ref, mid_ref, right_ref) for j in range(2)],
        axis=1,
    )
    hi = x.astype(BF16)
    rest = x - hi.astype(F32)
    mid = rest.astype(BF16)
    low = (rest - mid.astype(F32)).astype(BF16)
    y3 = jnp.dot(
        jnp.concatenate([low, mid, hi], axis=0), w_ref[...], preferred_element_type=F32
    )
    y = (y3[:rows] + y3[rows : 2 * rows]) + y3[2 * rows :]
    z = y[:, :512] + bias_ref[0:1, :]
    cand = jnp.tanh(y[:, 512:] + bias_ref[1:2, :])
    small = jnp.exp(-jnp.abs(z))
    big = 1.0 / (1.0 + small)
    small = small * big
    up = z >= 0
    retain = jnp.where(up, big, small)
    fresh = jnp.where(up, small, big) * cand
    order = [(il3, p) for il3 in range(4) for p in range(PD)]

    def cut(v, il3, p):
        return v[p * blocks : (p + 1) * blocks, il3 * 128 : (il3 + 1) * 128]

    dc = None
    for il3, p in order:
        d, o = cut(retain, il3, p), cut(fresh, il3, p)
        dc, oc = (d, o) if dc is None else (d * dc, d * oc + o)
    lane = lax.broadcasted_iota(jnp.int32, (blocks, 128), 1)
    sub = lax.broadcasted_iota(jnp.int32, (blocks, 128), 0)
    first = lane < 64
    od = pltpu.roll(dc, 64, 1)
    oo = pltpu.roll(oc, 64, 1)
    pd_all = dc * od
    po_all = jnp.where(first, od * oc + oo, dc * oo + oc)
    reach = 1
    while reach < blocks:
        sd = jnp.where(sub < reach, 1.0, pltpu.roll(pd_all, reach, 0))
        so = jnp.where(sub < reach, 0.0, pltpu.roll(po_all, reach, 0))
        po_all = pd_all * so + po_all
        pd_all = pd_all * sd
        reach *= 2
    before = jnp.where(sub < 1, 0.0, pltpu.roll(po_all, 1, 0))
    h = jnp.where(first, before, od * before + oo)
    states = {}
    for il3, p in order:
        h = cut(retain, il3, p) * h + cut(fresh, il3, p)
        states[il3, p] = h
    wide = jnp.concatenate(
        [jnp.concatenate([states[il3, p] for p in range(PD)], axis=1) for il3 in range(4)], axis=0
    )
    s = jnp.dot(wide, wo_ref[...], precision=lax.Precision.HIGHEST, preferred_element_type=F32)

    def over(op, v):
        v = jnp.broadcast_to(v, (8, 128))
        v = op(v, pltpu.roll(v, 2, 1))
        v = op(v, pltpu.roll(v, 4, 1))
        return op(v, pltpu.roll(v, 8, 1))[0:1]

    row = lax.broadcasted_iota(jnp.int32, (rows, 128), 0)
    col = lax.broadcasted_iota(jnp.int32, (rows, 128), 1)
    plane = (row % blocks) * 32 + ((col // 8) % 2) * 16 + (row // blocks) * 4 + (col % 8) // 2
    value = 1.0 / (0.1 + 0.9 * plane.astype(F32) / (PD * 8 * blocks - 1))
    highest = over(jnp.maximum, jnp.max(s, axis=0, keepdims=True))
    weights = jnp.exp(s - highest)
    total = over(jnp.add, jnp.sum(weights, axis=0, keepdims=True))
    depth = over(jnp.add, jnp.sum(weights * value, axis=0, keepdims=True))
    prob = weights / total
    expected = depth / total
    for u in range(2):
        mine = prob if u == 0 else pltpu.roll(prob, 120, 1)
        message = jnp.where(col < 8, mine, expected)
        for il3 in range(4):
            out_ref[pl.ds(u * 4 + il3, blocks, stride=8), :] = message[
                il3 * blocks : (il3 + 1) * blocks
            ]


def output_kernel(x_ref, prob_ref, map_ref):
    t = x_ref[...].T
    for p in range(PD):
        prob_ref[p] = t[p * 2 : p * 2 + 2]
    map_ref[...] = t[8:10]


def gate_rows(w_gates, slab):
    w = w_gates.reshape(3, 3, 2, 32, 8).transpose(0, 1, 4, 2, 3)
    w = jnp.pad(w, ((2, 2), (0, 0), (0, 0), (0, 0), (0, 0)))
    by_row = [lax.dynamic_slice_in_dim(w, 3 - r - 2 * slab, 4, axis=0) for r in range(2)]
    v = jnp.stack(by_row, axis=4).reshape(2, 2, 3, 8, 2, 2, 32)
    v = v.transpose(4, 2, 0, 1, 3, 5, 6).reshape(2, 96, 64)
    return jnp.concatenate([v, v], axis=2)


def body(ref_feat, src_feat, tile_owner, tile_local, col_shift, w_gates, bias_z, bias_c, w_out):
    owners = lax.axis_size("depth")
    row_count, feat, cols = ref_feat.shape
    requests = tile_local.shape[0]
    tiles = src_feat.shape[0]
    blocks = owners // 8
    message = jnp.concatenate(
        [tile_owner[:, 0], tile_local, col_shift, jnp.zeros((128 - 3 * requests,), jnp.int32)]
    )
    message = jnp.broadcast_to(message[None, None, :], (owners, 1, 128))
    asked = lax.all_to_all(message, "depth", split_axis=0, concat_axis=0, tiled=True)
    asked = asked.reshape(owners, 128)

    table, channels = pl.pallas_call(
        prepare_kernel,
        out_shape=(
            jax.ShapeDtypeStruct((row_count * (2 * MAXSHIFT + 1), feat, cols), F32),
            jax.ShapeDtypeStruct((tiles, feat, cols), BF16),
        ),
        in_specs=[vspec(), vspec()],
        out_specs=(vspec(), vspec()),
        scratch_shapes=[
            pltpu.VMEM((row_count * feat, cols), F32),
            pltpu.VMEM((tiles * feat, cols), F32),
        ],
        compiler_params=params(),
        cost_estimate=pl.CostEstimate(flops=2000000, transcendentals=0, bytes_accessed=4000000),
        name="prepare",
    )(ref_feat, src_feat)

    def answers_of(*refs):
        answer_kernel(requests, *refs)

    answers = pl.pallas_call(
        answers_of,
        out_shape=jax.ShapeDtypeStruct((cols * blocks, 128), F32),
        in_specs=[vspec(), vspec(), vspec()],
        out_specs=vspec(),
        scratch_shapes=[
            pltpu.VMEM((8, owners), jnp.int32),
            pltpu.SMEM((8, owners), jnp.int32),
            pltpu.SemaphoreType.DMA,
        ],
        compiler_params=params(),
        name="answer",
    )(asked, table, channels)
    answers = lax.all_to_all(
        answers.reshape(cols, blocks, 128), "depth", split_axis=0, concat_axis=0, tiled=True
    )

    slab = lax.axis_index("slab")

    def tables_of(*refs):
        table_kernel(requests, *refs)

    targets, gates = pl.pallas_call(
        tables_of,
        out_shape=(
            jax.ShapeDtypeStruct((owners, blocks, 128), F32),
            jax.ShapeDtypeStruct((768, 1024), BF16),
        ),
        in_specs=[vspec(), vspec()],
        out_specs=(vspec(), vspec()),
        scratch_shapes=[pltpu.VMEM((requests * blocks, 128), F32)],
        compiler_params=params(),
        cost_estimate=pl.CostEstimate(flops=20000000, transcendentals=0, bytes_accessed=3000000),
        name="tables",
    )(asked, gate_rows(w_gates, slab))

    cost = pl.pallas_call(
        combine_kernel,
        out_shape=jax.ShapeDtypeStruct((PD * blocks, 128), F32),
        in_specs=[vspec(), vspec()],
        out_specs=vspec(),
        compiler_params=params(),
        name="combine",
    )(answers, targets)
    both = lax.all_gather(cost, "slab", tiled=True)
    ends = owners - 1
    left = lax.ppermute(both, "depth", [(i, i + 1) for i in range(ends)])
    right = lax.ppermute(both, "depth", [(i + 1, i) for i in range(ends)])

    bias = jnp.stack([jnp.tile(bias_z, 16), jnp.tile(bias_c, 16)])
    unit_row = jnp.arange(512, dtype=jnp.int32)[:, None] // 32
    unit_row = ((unit_row // 2) % 2) * 8 + (unit_row // 4) * 2 + unit_row % 2
    score_col = jnp.arange(128, dtype=jnp.int32)[None, :] % 16
    project = jnp.where(unit_row == score_col, jnp.tile(w_out, 16)[:, None], 0.0)
    packed = pl.pallas_call(
        column_kernel,
        out_shape=jax.ShapeDtypeStruct((owners, 128), F32),
        in_specs=[vspec()] * 6,
        out_specs=vspec(),
        compiler_params=params(),
        name="column",
    )(left, both, right, gates, bias, project)
    packed = lax.all_to_all(
        packed.reshape(owners, 1, 128), "depth", split_axis=0, concat_axis=0, tiled=True
    )
    return pl.pallas_call(
        output_kernel,
        out_shape=(
            jax.ShapeDtypeStruct((PD, row_count, cols), F32),
            jax.ShapeDtypeStruct((row_count, cols), F32),
        ),
        in_specs=[vspec()],
        out_specs=(vspec(), vspec()),
        compiler_params=params(),
        name="output",
    )(packed.reshape(cols, 128))


def solution(mesh):
    return jax.shard_map(
        body,
        mesh=mesh,
        in_specs=(
            P("slab", None, None),
            P("depth", None, None),
            P(("depth", "slab"), None),
            P(("depth", "slab")),
            P(("depth", "slab")),
            P(),
            P(),
            P(),
            P(),
        ),
        out_specs=(P("depth", "slab", None), P("slab", None)),
        check_vma=False,
    )
```

```python
import jax
import jax.numpy as jnp
from jax import lax
from jax.experimental import pallas as pl
from jax.experimental.pallas import tpu as pltpu
from jax.sharding import PartitionSpec as P

VIEWS = 5
PD = 4
MAXSHIFT = 16
F32 = jnp.float32
BF16 = jnp.bfloat16
MIB = 1024 * 1024
TORUS = (4, 4, 8)


def params(mib):
    return pltpu.CompilerParams(vmem_limit_bytes=mib * MIB)


def line_bases():
    nx, ny, nz = TORUS
    return [(x * ny + (y - x) % ny) * nz for x in range(nx) for y in range(ny)]


def path():
    nz = TORUS[2]
    return [base + (n - m) % nz for m, base in enumerate(line_bases()) for n in range(nz)]


def vspec():
    return pl.BlockSpec(memory_space=pltpu.VMEM)


def sspec():
    return pl.BlockSpec(memory_space=pltpu.SMEM)


def prepare_kernel(ref_ref, src_ref, tab_ref, srce_ref, ref32, src32):
    rows, feat, cols = ref_ref.shape
    tiles = src_ref.shape[0]
    cpg = feat // 8
    for r in range(rows):
        ref32[pl.ds(r * feat, feat), :] = ref_ref[r].astype(F32)
    lane = lax.broadcasted_iota(jnp.int32, (8, cols), 1)
    for r in range(rows):
        for e in range(cpg):
            base = ref32[pl.ds(r * feat + e, 8, stride=cpg), :]
            for k in range(2 * MAXSHIFT + 1):
                shift = k - MAXSHIFT
                moved = base if shift == 0 else pltpu.roll(base, (-shift) % cols, 1)
                inside = (lane + shift >= 0) & (lane + shift < cols)
                tab_ref[r * (2 * MAXSHIFT + 1) + k, pl.ds(e * 8, 8), :] = jnp.where(inside, moved, 0.0)

    def widen(n, c):
        src32[pl.ds(n * feat, feat), :] = src_ref[n].astype(F32)
        return c

    lax.fori_loop(0, tiles, widen, 0, unroll=8)

    def reorder(n, c):
        parts = [src32[pl.ds(n * feat + e, 8, stride=cpg), :] for e in range(cpg)]
        srce_ref[n] = jnp.concatenate(parts, axis=0).astype(BF16)
        return c

    lax.fori_loop(0, tiles, reorder, 0, unroll=8)


def answer_kernel(requests, req_ref, tab_ref, srce_ref, out_ref, codes, table, sem):
    owners = req_ref.shape[0]
    cols = out_ref.shape[-1]
    me = lax.axis_index("depth")
    flat = req_ref[...].T
    owner = flat[0:requests]
    local = flat[requests : 2 * requests]
    shift = flat[2 * requests : 3 * requests]
    q = lax.broadcasted_iota(jnp.int32, (requests, owners), 0)
    hit = owner == me
    first = jnp.min(jnp.where(hit, q, requests), axis=0, keepdims=True)
    last = jnp.max(jnp.where(hit, q, -1), axis=0, keepdims=True)
    value = local + (shift + MAXSHIFT) * 256 + (q % 2) * 16384
    zero = jnp.zeros_like(value)
    code0 = jnp.sum(jnp.where(hit & (q == first), value, zero), axis=0, keepdims=True)
    code1 = jnp.sum(jnp.where(hit & (q == last) & (q > first), value, zero), axis=0, keepdims=True)
    sub = lax.broadcasted_iota(jnp.int32, (8, owners), 0)
    codes[...] = jnp.where(sub == 0, code0, jnp.where(sub == 1, code1, 0))
    copy = pltpu.make_async_copy(codes, table, sem)
    copy.start()
    copy.wait()

    def one(i, s):
        code = table[s, i]
        loc = code & 255
        moved = (code >> 8) & 63
        row = code >> 14
        tile = srce_ref[loc].astype(F32) * tab_ref[row * (2 * MAXSHIFT + 1) + moved]
        total = (tile[0:8] + tile[8:16]) + (tile[16:24] + tile[24:32])
        return pltpu.roll(total, (moved + cols - MAXSHIFT) % cols, 1)

    def step(b, c):
        parts = []
        for il in range(8):
            for s in range(2):
                parts.append(one(b * 8 + il, s))
        block = jnp.concatenate(parts, axis=0).T
        blocks = owners // 8
        for m, base in enumerate(line_bases()):
            turned = pltpu.roll(block[m * 8 : m * 8 + 8], (8 - m) % 8, 0)
            out_ref[pl.ds(base * blocks + b, 8, stride=blocks), :] = turned
        return c

    lax.fori_loop(0, owners // 8, step, 0, unroll=2)


def table_kernel(requests, req_ref, wd_ref, target_ref, gate_ref, keys):
    owners = req_ref.shape[0]
    blocks = owners // 8
    flat = req_ref[...].T
    owner = flat[0:requests]
    q = lax.broadcasted_iota(jnp.int32, (requests, owners), 0)
    earlier = jnp.zeros((requests, owners), jnp.int32)
    for other in range(requests - 1):
        same = (owner == owner[other : other + 1]) & (q > other)
        earlier = jnp.where(same, 1, earlier)
    key = (owner * 2 + earlier).astype(F32)
    block_row = lax.broadcasted_iota(jnp.int32, (blocks, owners), 0)
    block_of = lax.broadcasted_iota(jnp.int32, (blocks, owners), 1) // 8
    own_block = block_row == block_of
    spread = []
    for n in range(requests):
        row = jnp.broadcast_to(key[n : n + 1], (blocks, owners))
        spread.append(jnp.where(own_block, row, 0.0).astype(BF16))
    inner = lax.broadcasted_iota(jnp.int32, (owners, 128), 0) % 8
    lane = lax.broadcasted_iota(jnp.int32, (owners, 128), 1)
    pick = jnp.where(inner == lane // 16, 1.0, 0.0).astype(BF16)
    wide = jnp.dot(jnp.concatenate(spread, axis=0), pick, preferred_element_type=F32)
    slot = (lax.broadcasted_iota(jnp.int32, (blocks * requests, 128), 1) // 8) % 2
    keys[...] = wide - slot.astype(F32)

    def step(n, c):
        found = [[jnp.full((8, 128), 8.0, F32) for _ in range(blocks // 8)] for _ in range(4)]
        wanted = [(2 * (n * 4 + m)).astype(F32) for m in range(4)]
        for r in range(requests):
            t = float((r // (2 * VIEWS)) * 2 + r % 2)
            for half in range(blocks // 8):
                k = keys[r * blocks + half * 8 : r * blocks + half * 8 + 8, :]
                for m in range(4):
                    found[m][half] = jnp.where(k == wanted[m], t, found[m][half])
        for m in range(4):
            target_ref[n * 4 + m] = jnp.concatenate(found[m], axis=0).astype(BF16)
        return c

    lax.fori_loop(0, owners // 4, step, 0)

    half_of = lax.broadcasted_iota(jnp.int32, (16, 128), 1) // 64
    for source in range(6):
        for zc in range(2):
            part = wd_ref[zc, source * 16 : source * 16 + 16, :]
            for il in range(8):
                mine = jnp.where(half_of == il // 4, part, jnp.zeros_like(part))
                for il3 in range(4):
                    value = mine if il3 == il % 4 else jnp.zeros_like(part)
                    gate_ref[
                        pl.ds(source * 128 + il * 16, 16), pl.ds((zc * 4 + il3) * 128, 128)
                    ] = value


def combine_kernel(ans_ref, target_ref, out_ref):
    owners = ans_ref.shape[0]
    halves = ans_ref.shape[1] // 8

    def step(o, acc):
        acc = list(acc)
        targets = target_ref[o].astype(F32)
        for half in range(halves):
            data = ans_ref[o, half * 8 : half * 8 + 8, :]
            target = targets[half * 8 : half * 8 + 8, :]
            for t in range(8):
                n = t * halves + half
                acc[n] = acc[n] + jnp.where(target == float(t), data, 0.0)
        return tuple(acc)

    zero = jnp.zeros((8, 128), F32)
    acc = lax.fori_loop(0, owners, step, (zero,) * (8 * halves), unroll=8)
    lane = lax.broadcasted_iota(jnp.int32, (8, 128), 1)
    even = (lane // 8) % 2 == 0
    for p in range(PD):
        for half in range(halves):
            a = acc[(2 * p) * halves + half]
            b = acc[(2 * p + 1) * halves + half]
            a = a + pltpu.roll(a, 120, 1)
            b = b + pltpu.roll(b, 8, 1)
            out_ref[pl.ds((p * halves + half) * 8, 8), :] = jnp.where(even, a, b) / (VIEWS * 4.0)


def column_kernel(left_ref, mid_ref, right_ref, w_ref, bias_ref, wo_ref, out_ref):
    rows = mid_ref.shape[0] // 2
    blocks = rows // PD
    x = jnp.concatenate(
        [ref[pl.ds(j * rows, rows), :] for ref in (left_ref, mid_ref, right_ref) for j in range(2)],
        axis=1,
    )
    hi = x.astype(BF16)
    rest = x - hi.astype(F32)
    mid = rest.astype(BF16)
    low = (rest - mid.astype(F32)).astype(BF16)
    y3 = jnp.dot(
        jnp.concatenate([low, mid, hi], axis=0), w_ref[...], preferred_element_type=F32
    )
    y = (y3[:rows] + y3[rows : 2 * rows]) + y3[2 * rows :]
    z = y[:, :512] + bias_ref[0:1, :]
    cand = jnp.tanh(y[:, 512:] + bias_ref[1:2, :])
    small = jnp.exp(-jnp.abs(z))
    big = 1.0 / (1.0 + small)
    small = small * big
    up = z >= 0
    retain = jnp.where(up, big, small)
    fresh = jnp.where(up, small, big) * cand
    order = [(il3, p) for il3 in range(4) for p in range(PD)]

    def cut(v, il3, p):
        return v[p * blocks : (p + 1) * blocks, il3 * 128 : (il3 + 1) * 128]

    dc = None
    for il3, p in order:
        d, o = cut(retain, il3, p), cut(fresh, il3, p)
        dc, oc = (d, o) if dc is None else (d * dc, d * oc + o)
    lane = lax.broadcasted_iota(jnp.int32, (blocks, 128), 1)
    sub = lax.broadcasted_iota(jnp.int32, (blocks, 128), 0)
    first = lane < 64
    od = pltpu.roll(dc, 64, 1)
    oo = pltpu.roll(oc, 64, 1)
    pd_all = dc * od
    po_all = jnp.where(first, od * oc + oo, dc * oo + oc)
    reach = 1
    while reach < blocks:
        sd = jnp.where(sub < reach, 1.0, pltpu.roll(pd_all, reach, 0))
        so = jnp.where(sub < reach, 0.0, pltpu.roll(po_all, reach, 0))
        po_all = pd_all * so + po_all
        pd_all = pd_all * sd
        reach *= 2
    before = jnp.where(sub < 1, 0.0, pltpu.roll(po_all, 1, 0))
    h = jnp.where(first, before, od * before + oo)
    states = {}
    for il3, p in order:
        h = cut(retain, il3, p) * h + cut(fresh, il3, p)
        states[il3, p] = h
    wide = jnp.concatenate(
        [jnp.concatenate([states[il3, p] for p in range(PD)], axis=1) for il3 in range(4)], axis=0
    )
    s = jnp.dot(wide, wo_ref[...], precision=lax.Precision.HIGHEST, preferred_element_type=F32)

    def over(op, v):
        v = jnp.broadcast_to(v, (8, 128))
        v = op(v, pltpu.roll(v, 2, 1))
        v = op(v, pltpu.roll(v, 4, 1))
        return op(v, pltpu.roll(v, 8, 1))[0:1]

    row = lax.broadcasted_iota(jnp.int32, (rows, 128), 0)
    col = lax.broadcasted_iota(jnp.int32, (rows, 128), 1)
    plane = (row % blocks) * 32 + ((col // 8) % 2) * 16 + (row // blocks) * 4 + (col % 8) // 2
    value = 1.0 / (0.1 + 0.9 * plane.astype(F32) / (PD * 8 * blocks - 1))
    highest = over(jnp.maximum, jnp.max(s, axis=0, keepdims=True))
    weights = jnp.exp(s - highest)
    total = over(jnp.add, jnp.sum(weights, axis=0, keepdims=True))
    depth = over(jnp.add, jnp.sum(weights * value, axis=0, keepdims=True))
    prob = weights / total
    expected = depth / total
    for u in range(2):
        mine = prob if u == 0 else pltpu.roll(prob, 120, 1)
        message = jnp.where(col < 8, mine, expected)
        for il3 in range(4):
            out_ref[pl.ds(u * 4 + il3, blocks, stride=8), :] = message[
                il3 * blocks : (il3 + 1) * blocks
            ]


def output_kernel(x_ref, prob_ref, map_ref):
    lines = [pltpu.roll(x_ref[pl.ds(b, 8), :], m % 8, 0) for m, b in enumerate(line_bases())]
    t = jnp.concatenate(lines, axis=0).T
    for p in range(PD):
        prob_ref[p] = t[p * 2 : p * 2 + 2]
    map_ref[...] = t[8:10]


def gate_rows(w_gates, slab):
    w = w_gates.reshape(3, 3, 2, 32, 8).transpose(0, 1, 4, 2, 3)
    w = jnp.pad(w, ((2, 2), (0, 0), (0, 0), (0, 0), (0, 0)))
    by_row = [lax.dynamic_slice_in_dim(w, 3 - r - 2 * slab, 4, axis=0) for r in range(2)]
    v = jnp.stack(by_row, axis=4).reshape(2, 2, 3, 8, 2, 2, 32)
    v = v.transpose(4, 2, 0, 1, 3, 5, 6).reshape(2, 96, 64)
    return jnp.concatenate([v, v], axis=2)


def body(ref_feat, src_feat, tile_owner, tile_local, col_shift, w_gates, bias_z, bias_c, w_out):
    owners = lax.axis_size("depth")
    row_count, feat, cols = ref_feat.shape
    requests = tile_local.shape[0]
    tiles = src_feat.shape[0]
    blocks = owners // 8
    shape = (owners, 1, 128)
    message = jnp.where(
        lax.broadcasted_iota(jnp.int32, shape, 2) < 3 * requests,
        0,
        lax.broadcasted_iota(jnp.int32, shape, 0),
    )
    for n, part in enumerate((tile_owner[:, 0], tile_local, col_shift)):
        wide = jnp.broadcast_to(part[None, None, :], (owners, 1, requests))
        message += jnp.pad(wide, ((0, 0), (0, 0), (n * requests, 128 - (n + 1) * requests)))
    asked = lax.all_to_all(message, "depth", split_axis=0, concat_axis=0, tiled=True)
    asked = asked.reshape(owners, 128)

    table, channels = pl.pallas_call(
        prepare_kernel,
        out_shape=(
            jax.ShapeDtypeStruct((row_count * (2 * MAXSHIFT + 1), feat, cols), F32),
            jax.ShapeDtypeStruct((tiles, feat, cols), BF16),
        ),
        in_specs=[vspec(), vspec()],
        out_specs=(vspec(), vspec()),
        scratch_shapes=[
            pltpu.VMEM((row_count * feat, cols), F32),
            pltpu.VMEM((tiles * feat, cols), F32),
        ],
        compiler_params=params(16),
        cost_estimate=pl.CostEstimate(flops=2000000, transcendentals=0, bytes_accessed=4000000),
        name="prepare",
    )(ref_feat, src_feat)

    def answers_of(*refs):
        answer_kernel(requests, *refs)

    answers = pl.pallas_call(
        answers_of,
        out_shape=jax.ShapeDtypeStruct((cols * blocks, 128), F32),
        in_specs=[vspec(), vspec(), vspec()],
        out_specs=vspec(),
        scratch_shapes=[
            pltpu.VMEM((8, owners), jnp.int32),
            pltpu.SMEM((8, owners), jnp.int32),
            pltpu.SemaphoreType.DMA,
        ],
        compiler_params=params(10),
        name="answer",
    )(asked, table, channels)
    answers = lax.all_to_all(
        answers.reshape(cols, blocks, 128), "depth", split_axis=0, concat_axis=0, tiled=True
    )

    slab = lax.axis_index("slab")

    def tables_of(*refs):
        table_kernel(requests, *refs)

    targets, gates = pl.pallas_call(
        tables_of,
        out_shape=(
            jax.ShapeDtypeStruct((owners, blocks, 128), BF16),
            jax.ShapeDtypeStruct((768, 1024), BF16),
        ),
        in_specs=[vspec(), vspec()],
        out_specs=(vspec(), vspec()),
        scratch_shapes=[pltpu.VMEM((requests * blocks, 128), F32)],
        compiler_params=params(8),
        cost_estimate=pl.CostEstimate(flops=20000000, transcendentals=0, bytes_accessed=3000000),
        name="tables",
    )(asked, gate_rows(w_gates, slab))

    cost = pl.pallas_call(
        combine_kernel,
        out_shape=jax.ShapeDtypeStruct((PD * blocks, 128), F32),
        in_specs=[vspec(), vspec()],
        out_specs=vspec(),
        compiler_params=params(6),
        name="combine",
    )(answers, targets)
    both = lax.all_gather(cost, "slab", tiled=True)
    chips = path()
    pairs = list(zip(chips[:-1], chips[1:]))
    left = lax.ppermute(both, "depth", pairs)
    right = lax.ppermute(both, "depth", [(b, a) for a, b in pairs])

    bias = jnp.stack([jnp.tile(bias_z, 16), jnp.tile(bias_c, 16)])
    unit_row = jnp.arange(512, dtype=jnp.int32)[:, None] // 32
    unit_row = ((unit_row // 2) % 2) * 8 + (unit_row // 4) * 2 + unit_row % 2
    score_col = jnp.arange(128, dtype=jnp.int32)[None, :] % 16
    project = jnp.where(unit_row == score_col, jnp.tile(w_out, 16)[:, None], 0.0)
    packed = pl.pallas_call(
        column_kernel,
        out_shape=jax.ShapeDtypeStruct((owners, 128), F32),
        in_specs=[vspec()] * 6,
        out_specs=vspec(),
        compiler_params=params(10),
        name="column",
    )(left, both, right, gates, bias, project)
    packed = lax.all_to_all(
        packed.reshape(owners, 1, 128), "depth", split_axis=0, concat_axis=0, tiled=True
    )
    return pl.pallas_call(
        output_kernel,
        out_shape=(
            jax.ShapeDtypeStruct((PD, row_count, cols), F32),
            jax.ShapeDtypeStruct((row_count, cols), F32),
        ),
        in_specs=[vspec()],
        out_specs=(vspec(), vspec()),
        compiler_params=params(4),
        name="output",
    )(packed.reshape(cols, 128))


def solution(mesh):
    return jax.shard_map(
        body,
        mesh=mesh,
        in_specs=(
            P("slab", None, None),
            P("depth", None, None),
            P(("depth", "slab"), None),
            P(("depth", "slab")),
            P(("depth", "slab")),
            P(),
            P(),
            P(),
            P(),
        ),
        out_specs=(P("depth", "slab", None), P("slab", None)),
        check_vma=False,
    )
```

```python
import jax
import jax.numpy as jnp
from jax import lax
from jax.experimental import pallas as pl
from jax.experimental.pallas import tpu as pltpu
from jax.sharding import PartitionSpec as P

VIEWS = 5
STEPS = 16384.0
PD = 4
MAXSHIFT = 16
F32 = jnp.float32
BF16 = jnp.bfloat16
UNROLL = 4
MIB = 1024 * 1024
TORUS = (4, 4, 8)


def params(mib):
    return pltpu.CompilerParams(vmem_limit_bytes=mib * MIB)


def line_bases():
    nx, ny, nz = TORUS
    return [(x * ny + (y - x) % ny) * nz for x in range(nx) for y in range(ny)]


def path():
    nz = TORUS[2]
    return [base + (n - m) % nz for m, base in enumerate(line_bases()) for n in range(nz)]


def message_kernel(a_ref, b_ref, c_ref, out_ref, a_s, b_s, c_s, sems):
    copies = [
        pltpu.make_async_copy(ref, scratch, sems.at[n])
        for n, (ref, scratch) in enumerate(((a_ref, a_s), (b_ref, b_s), (c_ref, c_s)))
    ]
    for copy in copies:
        copy.start()
    for copy in copies:
        copy.wait()
    rest = jnp.zeros((1, 128 - 3 * a_s.shape[1]), jnp.int32)
    row = jnp.concatenate([a_s[...], b_s[...], c_s[...], rest], axis=1)
    out_ref[...] = jnp.broadcast_to(row, out_ref.shape)


def vspec():
    return pl.BlockSpec(memory_space=pltpu.VMEM)


def sspec():
    return pl.BlockSpec(memory_space=pltpu.SMEM)


def prepare_kernel(ref_ref, src_ref, tab_ref, srce_ref, ref32, src32):
    rows, feat, cols = ref_ref.shape
    tiles = src_ref.shape[0]
    cpg = feat // 8
    for r in range(rows):
        ref32[pl.ds(r * feat, feat), :] = ref_ref[r].astype(F32)
    lane = lax.broadcasted_iota(jnp.int32, (8, cols), 1)
    for r in range(rows):
        for e in range(cpg):
            base = ref32[pl.ds(r * feat + e, 8, stride=cpg), :]
            for k in range(2 * MAXSHIFT + 1):
                shift = k - MAXSHIFT
                moved = base if shift == 0 else pltpu.roll(base, (-shift) % cols, 1)
                inside = (lane + shift >= 0) & (lane + shift < cols)
                tab_ref[r * (2 * MAXSHIFT + 1) + k, pl.ds(e * 8, 8), :] = jnp.where(inside, moved, 0.0)

    def widen(n, c):
        src32[pl.ds(n * feat, feat), :] = src_ref[n].astype(F32)
        return c

    lax.fori_loop(0, tiles, widen, 0, unroll=8)

    def reorder(n, c):
        parts = [src32[pl.ds(n * feat + e, 8, stride=cpg), :] for e in range(cpg)]
        srce_ref[n] = jnp.concatenate(parts, axis=0).astype(BF16)
        return c

    lax.fori_loop(0, tiles, reorder, 0, unroll=8)


def answer_kernel(requests, req_ref, tab_ref, srce_ref, out_ref, flat_s, codes, table, sem):
    owners = req_ref.shape[0]
    cols = tab_ref.shape[-1]
    blocks = owners // 8
    me = lax.axis_index("depth")
    flat = req_ref[...].T
    owner = flat[0:requests]
    local = flat[requests : 2 * requests]
    shift = flat[2 * requests : 3 * requests]
    q = lax.broadcasted_iota(jnp.int32, (requests, owners), 0)
    hit = owner == me
    first = jnp.min(jnp.where(hit, q, requests), axis=0, keepdims=True)
    last = jnp.max(jnp.where(hit, q, -1), axis=0, keepdims=True)
    value = local + (shift + MAXSHIFT) * 256 + (q % 2) * 16384
    zero = jnp.zeros_like(value)
    code0 = jnp.sum(jnp.where(hit & (q == first), value, zero), axis=0, keepdims=True)
    code1 = jnp.sum(jnp.where(hit & (q == last) & (q > first), value, zero), axis=0, keepdims=True)
    sub = lax.broadcasted_iota(jnp.int32, (8, owners), 0)
    codes[...] = jnp.where(sub == 0, code0, jnp.where(sub == 1, code1, 0))
    copy = pltpu.make_async_copy(codes, table, sem)
    copy.start()
    copy.wait()

    def one(i, s):
        code = table[s, i]
        loc = code & 255
        moved = (code >> 8) & 63
        row = code >> 14
        tile = srce_ref[loc].astype(F32) * tab_ref[row * (2 * MAXSHIFT + 1) + moved]
        total = (tile[0:8] + tile[8:16]) + (tile[16:24] + tile[24:32])
        return pltpu.roll(total, (moved + cols - MAXSHIFT) % cols, 1)

    def step(b, c):
        parts = []
        for il in range(8):
            for s in range(2):
                parts.append(one(b * 8 + il, s))
        block = jnp.concatenate(parts, axis=0).T
        for m, base in enumerate(line_bases()):
            turned = pltpu.roll(block[m * 8 : m * 8 + 8], (8 - m) % 8, 0)
            flat_s[pl.ds(base * blocks + b, 8, stride=blocks), :] = turned
        return c

    lax.fori_loop(0, blocks, step, 0, unroll=UNROLL)

    def encode(k, c):
        number = jnp.round(flat_s[pl.ds(k * blocks, blocks), :] * STEPS).astype(jnp.int32)
        low = number & 255
        out_ref[k, 0:blocks, :] = (number >> 8).astype(jnp.int16)
        pair = low[: blocks // 2] * 256 + low[blocks // 2 :] - 32768
        out_ref[k, blocks : blocks + blocks // 2, :] = pair.astype(jnp.int16)
        return c

    lax.fori_loop(0, cols, encode, 0, unroll=8)


def table_kernel(requests, req_ref, wd_ref, target_ref, gate_ref, keys):
    owners = req_ref.shape[0]
    blocks = owners // 8
    flat = req_ref[...].T
    owner = flat[0:requests]
    q = lax.broadcasted_iota(jnp.int32, (requests, owners), 0)
    earlier = jnp.zeros((requests, owners), jnp.int32)
    for other in range(requests - 1):
        same = (owner == owner[other : other + 1]) & (q > other)
        earlier = jnp.where(same, 1, earlier)
    key = (owner * 2 + earlier).astype(F32)
    block_row = lax.broadcasted_iota(jnp.int32, (blocks, owners), 0)
    block_of = lax.broadcasted_iota(jnp.int32, (blocks, owners), 1) // 8
    own_block = block_row == block_of
    spread = []
    for n in range(requests):
        row = jnp.broadcast_to(key[n : n + 1], (blocks, owners))
        spread.append(jnp.where(own_block, row, 0.0).astype(BF16))
    inner = lax.broadcasted_iota(jnp.int32, (owners, 128), 0) % 8
    lane = lax.broadcasted_iota(jnp.int32, (owners, 128), 1)
    pick = jnp.where(inner == lane // 16, 1.0, 0.0).astype(BF16)
    wide = jnp.dot(jnp.concatenate(spread, axis=0), pick, preferred_element_type=F32)
    slot = (lax.broadcasted_iota(jnp.int32, (blocks * requests, 128), 1) // 8) % 2
    keys[...] = wide - slot.astype(F32)

    def step(n, c):
        found = [[jnp.full((8, 128), 8.0, F32) for _ in range(blocks // 8)] for _ in range(4)]
        wanted = [(2 * (n * 4 + m)).astype(F32) for m in range(4)]
        for r in range(requests):
            t = float((r // (2 * VIEWS)) * 2 + r % 2)
            for half in range(blocks // 8):
                k = keys[r * blocks + half * 8 : r * blocks + half * 8 + 8, :]
                for m in range(4):
                    found[m][half] = jnp.where(k == wanted[m], t, found[m][half])
        for m in range(4):
            target_ref[n * 4 + m] = jnp.concatenate(found[m], axis=0).astype(BF16)
        return c

    lax.fori_loop(0, owners // 4, step, 0)

    half_of = lax.broadcasted_iota(jnp.int32, (16, 128), 1) // 64
    for source in range(6):
        for zc in range(2):
            part = wd_ref[zc, source * 16 : source * 16 + 16, :]
            for il in range(8):
                mine = jnp.where(half_of == il // 4, part, jnp.zeros_like(part))
                for il3 in range(4):
                    value = mine if il3 == il % 4 else jnp.zeros_like(part)
                    gate_ref[
                        pl.ds(source * 128 + il * 16, 16), pl.ds((zc * 4 + il3) * 128, 128)
                    ] = value


def combine_kernel(ans_ref, target_ref, out_ref):
    owners = ans_ref.shape[0]
    halves = target_ref.shape[1] // 8

    def step(o, acc):
        acc = list(acc)
        targets = target_ref[o].astype(F32)
        high = ans_ref[o, 0 : halves * 8, :].astype(jnp.int32)
        pair = ans_ref[o, halves * 8 : halves * 12, :].astype(jnp.int32) + 32768
        number = high * 256 + jnp.concatenate([pair >> 8, pair & 255], axis=0)
        number = number.astype(F32)
        for half in range(halves):
            data = number[half * 8 : half * 8 + 8]
            target = targets[half * 8 : half * 8 + 8, :]
            for t in range(8):
                n = t * halves + half
                acc[n] = acc[n] + jnp.where(target == float(t), data, 0.0)
        return tuple(acc)

    zero = jnp.zeros((8, 128), F32)
    acc = lax.fori_loop(0, owners, step, (zero,) * (8 * halves), unroll=8)
    lane = lax.broadcasted_iota(jnp.int32, (8, 128), 1)
    even = (lane // 8) % 2 == 0
    for p in range(PD):
        for half in range(halves):
            a = acc[(2 * p) * halves + half]
            b = acc[(2 * p + 1) * halves + half]
            a = a + pltpu.roll(a, 120, 1)
            b = b + pltpu.roll(b, 8, 1)
            out_ref[pl.ds((p * halves + half) * 8, 8), :] = jnp.where(even, a, b) / (
                VIEWS * 4.0 * STEPS
            )


def column_kernel(left_ref, mid_ref, right_ref, w_ref, bias_ref, wo_ref, out_ref):
    rows = mid_ref.shape[0] // 2
    blocks = rows // PD
    x = jnp.concatenate(
        [ref[pl.ds(j * rows, rows), :] for ref in (left_ref, mid_ref, right_ref) for j in range(2)],
        axis=1,
    )
    hi = x.astype(BF16)
    rest = x - hi.astype(F32)
    mid = rest.astype(BF16)
    low = (rest - mid.astype(F32)).astype(BF16)
    y3 = jnp.dot(
        jnp.concatenate([low, mid, hi], axis=0), w_ref[...], preferred_element_type=F32
    )
    y = (y3[:rows] + y3[rows : 2 * rows]) + y3[2 * rows :]
    z = y[:, :512] + bias_ref[0:1, :]
    cand = jnp.tanh(y[:, 512:] + bias_ref[1:2, :])
    small = jnp.exp(-jnp.abs(z))
    big = 1.0 / (1.0 + small)
    small = small * big
    up = z >= 0
    retain = jnp.where(up, big, small)
    fresh = jnp.where(up, small, big) * cand
    order = [(il3, p) for il3 in range(4) for p in range(PD)]

    def cut(v, il3, p):
        return v[p * blocks : (p + 1) * blocks, il3 * 128 : (il3 + 1) * 128]

    dc = None
    for il3, p in order:
        d, o = cut(retain, il3, p), cut(fresh, il3, p)
        dc, oc = (d, o) if dc is None else (d * dc, d * oc + o)
    lane = lax.broadcasted_iota(jnp.int32, (blocks, 128), 1)
    sub = lax.broadcasted_iota(jnp.int32, (blocks, 128), 0)
    first = lane < 64
    od = pltpu.roll(dc, 64, 1)
    oo = pltpu.roll(oc, 64, 1)
    pd_all = dc * od
    po_all = jnp.where(first, od * oc + oo, dc * oo + oc)
    reach = 1
    while reach < blocks:
        sd = jnp.where(sub < reach, 1.0, pltpu.roll(pd_all, reach, 0))
        so = jnp.where(sub < reach, 0.0, pltpu.roll(po_all, reach, 0))
        po_all = pd_all * so + po_all
        pd_all = pd_all * sd
        reach *= 2
    before = jnp.where(sub < 1, 0.0, pltpu.roll(po_all, 1, 0))
    h = jnp.where(first, before, od * before + oo)
    states = {}
    for il3, p in order:
        h = cut(retain, il3, p) * h + cut(fresh, il3, p)
        states[il3, p] = h
    wide = jnp.concatenate(
        [jnp.concatenate([states[il3, p] for p in range(PD)], axis=1) for il3 in range(4)], axis=0
    )
    s = jnp.dot(wide, wo_ref[...], precision=lax.Precision.HIGHEST, preferred_element_type=F32)

    def over(op, v):
        v = jnp.broadcast_to(v, (8, 128))
        v = op(v, pltpu.roll(v, 2, 1))
        v = op(v, pltpu.roll(v, 4, 1))
        return op(v, pltpu.roll(v, 8, 1))[0:1]

    row = lax.broadcasted_iota(jnp.int32, (rows, 128), 0)
    col = lax.broadcasted_iota(jnp.int32, (rows, 128), 1)
    plane = (row % blocks) * 32 + ((col // 8) % 2) * 16 + (row // blocks) * 4 + (col % 8) // 2
    value = 1.0 / (0.1 + 0.9 * plane.astype(F32) / (PD * 8 * blocks - 1))
    highest = over(jnp.maximum, jnp.max(s, axis=0, keepdims=True))
    weights = jnp.exp(s - highest)
    total = over(jnp.add, jnp.sum(weights, axis=0, keepdims=True))
    depth = over(jnp.add, jnp.sum(weights * value, axis=0, keepdims=True))
    prob = weights / total
    expected = depth / total
    for u in range(2):
        mine = prob if u == 0 else pltpu.roll(prob, 120, 1)
        message = jnp.where(col < 8, mine, expected)
        for il3 in range(4):
            out_ref[pl.ds(u * 4 + il3, blocks, stride=8), :] = message[
                il3 * blocks : (il3 + 1) * blocks
            ]


def output_kernel(x_ref, prob_ref, map_ref):
    lines = [pltpu.roll(x_ref[pl.ds(b, 8), :], m % 8, 0) for m, b in enumerate(line_bases())]
    t = jnp.concatenate(lines, axis=0).T
    for p in range(PD):
        prob_ref[p] = t[p * 2 : p * 2 + 2]
    map_ref[...] = t[8:10]


def gate_rows(w_gates, slab):
    w = w_gates.reshape(3, 3, 2, 32, 8).transpose(0, 1, 4, 2, 3)
    w = jnp.pad(w, ((2, 2), (0, 0), (0, 0), (0, 0), (0, 0)))
    by_row = [lax.dynamic_slice_in_dim(w, 3 - r - 2 * slab, 4, axis=0) for r in range(2)]
    v = jnp.stack(by_row, axis=4).reshape(2, 2, 3, 8, 2, 2, 32)
    v = v.transpose(4, 2, 0, 1, 3, 5, 6).reshape(2, 96, 64)
    return jnp.concatenate([v, v], axis=2)


def body(ref_feat, src_feat, tile_owner, tile_local, col_shift, w_gates, bias_z, bias_c, w_out):
    owners = lax.axis_size("depth")
    row_count, feat, cols = ref_feat.shape
    requests = tile_local.shape[0]
    tiles = src_feat.shape[0]
    blocks = owners // 8
    message = pl.pallas_call(
        message_kernel,
        out_shape=jax.ShapeDtypeStruct((owners, 128), jnp.int32),
        in_specs=[pl.BlockSpec(memory_space=pltpu.HBM)] * 3,
        out_specs=vspec(),
        scratch_shapes=[pltpu.VMEM((1, requests), jnp.int32)] * 3 + [pltpu.SemaphoreType.DMA((3,))],
        compiler_params=params(60),
        name="message",
    )(*[v.reshape(1, requests) for v in (tile_owner, tile_local, col_shift)])
    message = message.reshape(owners, 1, 128)
    asked = lax.all_to_all(message, "depth", split_axis=0, concat_axis=0, tiled=True)
    asked = asked.reshape(owners, 128)

    table, channels = pl.pallas_call(
        prepare_kernel,
        out_shape=(
            jax.ShapeDtypeStruct((row_count * (2 * MAXSHIFT + 1), feat, cols), F32),
            jax.ShapeDtypeStruct((tiles, feat, cols), BF16),
        ),
        in_specs=[vspec(), vspec()],
        out_specs=(vspec(), vspec()),
        scratch_shapes=[
            pltpu.VMEM((row_count * feat, cols), F32),
            pltpu.VMEM((tiles * feat, cols), F32),
        ],
        compiler_params=params(16),
        cost_estimate=pl.CostEstimate(flops=2000000, transcendentals=0, bytes_accessed=4000000),
        name="prepare",
    )(ref_feat, src_feat)

    def answers_of(*refs):
        answer_kernel(requests, *refs)

    answers = pl.pallas_call(
        answers_of,
        out_shape=jax.ShapeDtypeStruct((cols, blocks + blocks // 2, 128), jnp.int16),
        in_specs=[vspec(), vspec(), vspec()],
        out_specs=vspec(),
        scratch_shapes=[
            pltpu.VMEM((cols * blocks, 128), F32),
            pltpu.VMEM((8, owners), jnp.int32),
            pltpu.SMEM((8, owners), jnp.int32),
            pltpu.SemaphoreType.DMA,
        ],
        compiler_params=params(10),
        name="answer",
    )(asked, table, channels)
    answers = lax.all_to_all(answers, "depth", split_axis=0, concat_axis=0, tiled=True)

    slab = lax.axis_index("slab")

    def tables_of(*refs):
        table_kernel(requests, *refs)

    targets, gates = pl.pallas_call(
        tables_of,
        out_shape=(
            jax.ShapeDtypeStruct((owners, blocks, 128), BF16),
            jax.ShapeDtypeStruct((768, 1024), BF16),
        ),
        in_specs=[vspec(), vspec()],
        out_specs=(vspec(), vspec()),
        scratch_shapes=[pltpu.VMEM((requests * blocks, 128), F32)],
        compiler_params=params(8),
        cost_estimate=pl.CostEstimate(flops=20000000, transcendentals=0, bytes_accessed=3000000),
        name="tables",
    )(asked, gate_rows(w_gates, slab))

    cost = pl.pallas_call(
        combine_kernel,
        out_shape=jax.ShapeDtypeStruct((PD * blocks, 128), F32),
        in_specs=[vspec(), vspec()],
        out_specs=vspec(),
        compiler_params=params(6),
        name="combine",
    )(answers, targets)
    both = lax.all_gather(cost, "slab", tiled=True)
    chips = path()
    pairs = list(zip(chips[:-1], chips[1:]))
    left = lax.ppermute(both, "depth", pairs)
    right = lax.ppermute(both, "depth", [(b, a) for a, b in pairs])

    bias = jnp.stack([jnp.tile(bias_z, 16), jnp.tile(bias_c, 16)])
    unit_row = jnp.arange(512, dtype=jnp.int32)[:, None] // 32
    unit_row = ((unit_row // 2) % 2) * 8 + (unit_row // 4) * 2 + unit_row % 2
    score_col = jnp.arange(128, dtype=jnp.int32)[None, :] % 16
    project = jnp.where(unit_row == score_col, jnp.tile(w_out, 16)[:, None], 0.0)
    packed = pl.pallas_call(
        column_kernel,
        out_shape=jax.ShapeDtypeStruct((owners, 128), F32),
        in_specs=[vspec()] * 6,
        out_specs=vspec(),
        compiler_params=params(10),
        name="column",
    )(left, both, right, gates, bias, project)
    packed = lax.all_to_all(
        packed.reshape(owners, 1, 128), "depth", split_axis=0, concat_axis=0, tiled=True
    )
    return pl.pallas_call(
        output_kernel,
        out_shape=(
            jax.ShapeDtypeStruct((PD, row_count, cols), F32),
            jax.ShapeDtypeStruct((row_count, cols), F32),
        ),
        in_specs=[vspec()],
        out_specs=(vspec(), vspec()),
        compiler_params=params(4),
        name="output",
    )(packed.reshape(cols, 128))


def solution(mesh):
    return jax.shard_map(
        body,
        mesh=mesh,
        in_specs=(
            P("slab", None, None),
            P("depth", None, None),
            P(("depth", "slab"), None),
            P(("depth", "slab")),
            P(("depth", "slab")),
            P(),
            P(),
            P(),
            P(),
        ),
        out_specs=(P("depth", "slab", None), P("slab", None)),
        check_vma=False,
    )
```

```python
import jax
import jax.numpy as jnp
from jax import lax
from jax.experimental import pallas as pl
from jax.experimental.pallas import tpu as pltpu
from jax.sharding import PartitionSpec as P

VIEWS = 5
STEPS = 16384.0
PD = 4
MAXSHIFT = 16
F32 = jnp.float32
BF16 = jnp.bfloat16
UNROLL = 4
PIECES = 4
MIB = 1024 * 1024
TORUS = (4, 4, 8)


def params(mib):
    return pltpu.CompilerParams(vmem_limit_bytes=mib * MIB)


def column_of(k):
    nx, ny, nz = TORUS
    x, y, z = k // (ny * nz), (k // nz) % ny, k % nz
    line = x * ny + y + (x % 2) * (ny - 1 - 2 * y)
    return line * nz + z + (line % 2) * (nz - 1 - 2 * z)


def path():
    return sorted(range(TORUS[0] * TORUS[1] * TORUS[2]), key=column_of)


def message_kernel(a_ref, b_ref, c_ref, out_ref, a_s, b_s, c_s, sems):
    copies = [
        pltpu.make_async_copy(ref, scratch, sems.at[n])
        for n, (ref, scratch) in enumerate(((a_ref, a_s), (b_ref, b_s), (c_ref, c_s)))
    ]
    for copy in copies:
        copy.start()
    for copy in copies:
        copy.wait()
    rest = jnp.zeros((1, 128 - 3 * a_s.shape[1]), jnp.int32)
    row = jnp.concatenate([a_s[...], b_s[...], c_s[...], rest], axis=1)
    out_ref[...] = jnp.broadcast_to(row, out_ref.shape)


def vspec():
    return pl.BlockSpec(memory_space=pltpu.VMEM)


def sspec():
    return pl.BlockSpec(memory_space=pltpu.SMEM)


def prepare_kernel(ref_ref, src_ref, tab_ref, srce_ref, ref32, src32):
    rows, feat, cols = ref_ref.shape
    tiles = src_ref.shape[0]
    cpg = feat // 8
    for r in range(rows):
        ref32[pl.ds(r * feat, feat), :] = ref_ref[r].astype(F32)
    lane = lax.broadcasted_iota(jnp.int32, (8, cols), 1)
    for r in range(rows):
        for e in range(cpg):
            base = ref32[pl.ds(r * feat + e, 8, stride=cpg), :]
            for k in range(2 * MAXSHIFT + 1):
                shift = k - MAXSHIFT
                moved = base if shift == 0 else pltpu.roll(base, (-shift) % cols, 1)
                inside = (lane + shift >= 0) & (lane + shift < cols)
                tab_ref[r * (2 * MAXSHIFT + 1) + k, pl.ds(e * 8, 8), :] = jnp.where(inside, moved, 0.0)

    def widen(n, c):
        src32[pl.ds(n * feat, feat), :] = src_ref[n].astype(F32)
        return c

    lax.fori_loop(0, tiles, widen, 0, unroll=8)

    def reorder(n, c):
        parts = [src32[pl.ds(n * feat + e, 8, stride=cpg), :] for e in range(cpg)]
        srce_ref[n] = jnp.concatenate(parts, axis=0).astype(BF16)
        return c

    lax.fori_loop(0, tiles, reorder, 0, unroll=8)


def answer_kernel(requests, req_ref, tab_ref, srce_ref, out_ref, flat_s, coded_s, codes, table, sem, out_sem):
    owners = req_ref.shape[0]
    cols = tab_ref.shape[-1]
    blocks = owners // 8
    me = lax.axis_index("depth")
    flat = req_ref[...].T
    owner = flat[0:requests]
    local = flat[requests : 2 * requests]
    shift = flat[2 * requests : 3 * requests]
    q = lax.broadcasted_iota(jnp.int32, (requests, owners), 0)
    hit = owner == me
    first = jnp.min(jnp.where(hit, q, requests), axis=0, keepdims=True)
    last = jnp.max(jnp.where(hit, q, -1), axis=0, keepdims=True)
    value = local + (shift + MAXSHIFT) * 256 + (q % 2) * 16384
    zero = jnp.zeros_like(value)
    code0 = jnp.sum(jnp.where(hit & (q == first), value, zero), axis=0, keepdims=True)
    code1 = jnp.sum(jnp.where(hit & (q == last) & (q > first), value, zero), axis=0, keepdims=True)
    sub = lax.broadcasted_iota(jnp.int32, (8, owners), 0)
    codes[...] = jnp.where(sub == 0, code0, jnp.where(sub == 1, code1, 0))
    copy = pltpu.make_async_copy(codes, table, sem)
    copy.start()
    copy.wait()

    def one(i, s):
        code = table[s, i]
        loc = code & 255
        moved = (code >> 8) & 63
        row = code >> 14
        tile = srce_ref[loc].astype(F32) * tab_ref[row * (2 * MAXSHIFT + 1) + moved]
        total = (tile[0:8] + tile[8:16]) + (tile[16:24] + tile[24:32])
        return pltpu.roll(total, (moved + cols - MAXSHIFT) % cols, 1)

    def step(b, c):
        parts = []
        for il in range(8):
            for s in range(2):
                parts.append(one(b * 8 + il, s))
        flat_s[pl.ds(b, cols, stride=blocks), :] = jnp.concatenate(parts, axis=0).T
        return c

    lax.fori_loop(0, blocks, step, 0, unroll=UNROLL)

    def encode(k, c):
        start = pl.multiple_of(column_of(k) * blocks, blocks)
        number = jnp.round(flat_s[pl.ds(start, blocks), :] * STEPS).astype(jnp.int32)
        low = number & 255
        coded_s[k, 0:blocks, :] = (number >> 8).astype(jnp.int16)
        pair = low[: blocks // 2] * 256 + low[blocks // 2 :] - 32768
        coded_s[k, blocks : blocks + blocks // 2, :] = pair.astype(jnp.int16)
        return c

    size = cols // PIECES
    copies = []
    for n in range(PIECES):
        lax.fori_loop(n * size, (n + 1) * size, encode, 0, unroll=8)
        piece = pl.ds(n * size, size)
        copies.append(pltpu.make_async_copy(coded_s.at[piece], out_ref.at[piece], out_sem.at[n]))
        copies[-1].start()
    for copy in copies:
        copy.wait()


def table_kernel(requests, req_ref, wd_ref, target_ref, gate_ref, keys):
    owners = req_ref.shape[0]
    blocks = owners // 8
    flat = req_ref[...].T
    owner = flat[0:requests]
    q = lax.broadcasted_iota(jnp.int32, (requests, owners), 0)
    earlier = jnp.zeros((requests, owners), jnp.int32)
    for other in range(requests - 1):
        same = (owner == owner[other : other + 1]) & (q > other)
        earlier = jnp.where(same, 1, earlier)
    key = (owner * 2 + earlier).astype(F32)
    block_row = lax.broadcasted_iota(jnp.int32, (blocks, owners), 0)
    block_of = lax.broadcasted_iota(jnp.int32, (blocks, owners), 1) // 8
    own_block = block_row == block_of
    spread = []
    for n in range(requests):
        row = jnp.broadcast_to(key[n : n + 1], (blocks, owners))
        spread.append(jnp.where(own_block, row, 0.0).astype(BF16))
    inner = lax.broadcasted_iota(jnp.int32, (owners, 128), 0) % 8
    lane = lax.broadcasted_iota(jnp.int32, (owners, 128), 1)
    pick = jnp.where(inner == lane // 16, 1.0, 0.0).astype(BF16)
    wide = jnp.dot(jnp.concatenate(spread, axis=0), pick, preferred_element_type=F32)
    slot = (lax.broadcasted_iota(jnp.int32, (blocks * requests, 128), 1) // 8) % 2
    keys[...] = wide - slot.astype(F32)

    def step(n, c):
        found = [[jnp.full((8, 128), 8.0, F32) for _ in range(blocks // 8)] for _ in range(4)]
        wanted = [(2 * (n * 4 + m)).astype(F32) for m in range(4)]
        for r in range(requests):
            t = float((r // (2 * VIEWS)) * 2 + r % 2)
            for half in range(blocks // 8):
                k = keys[r * blocks + half * 8 : r * blocks + half * 8 + 8, :]
                for m in range(4):
                    found[m][half] = jnp.where(k == wanted[m], t, found[m][half])
        for m in range(4):
            target_ref[n * 4 + m] = jnp.concatenate(found[m], axis=0).astype(BF16)
        return c

    lax.fori_loop(0, owners // 4, step, 0)

    half_of = lax.broadcasted_iota(jnp.int32, (16, 128), 1) // 64
    for source in range(6):
        for zc in range(2):
            part = wd_ref[zc, source * 16 : source * 16 + 16, :]
            for il in range(8):
                mine = jnp.where(half_of == il // 4, part, jnp.zeros_like(part))
                for il3 in range(4):
                    value = mine if il3 == il % 4 else jnp.zeros_like(part)
                    gate_ref[
                        pl.ds(source * 128 + il * 16, 16), pl.ds((zc * 4 + il3) * 128, 128)
                    ] = value


def combine_kernel(ans_ref, target_ref, out_ref):
    owners = ans_ref.shape[0]
    halves = target_ref.shape[1] // 8

    def step(o, acc):
        acc = list(acc)
        targets = target_ref[o].astype(F32)
        high = ans_ref[o, 0 : halves * 8, :].astype(jnp.int32)
        pair = ans_ref[o, halves * 8 : halves * 12, :].astype(jnp.int32) + 32768
        number = high * 256 + jnp.concatenate([pair >> 8, pair & 255], axis=0)
        number = number.astype(F32)
        for half in range(halves):
            data = number[half * 8 : half * 8 + 8]
            target = targets[half * 8 : half * 8 + 8, :]
            for t in range(8):
                n = t * halves + half
                acc[n] = acc[n] + jnp.where(target == float(t), data, 0.0)
        return tuple(acc)

    zero = jnp.zeros((8, 128), F32)
    acc = lax.fori_loop(0, owners, step, (zero,) * (8 * halves), unroll=8)
    lane = lax.broadcasted_iota(jnp.int32, (8, 128), 1)
    even = (lane // 8) % 2 == 0
    for p in range(PD):
        for half in range(halves):
            a = acc[(2 * p) * halves + half]
            b = acc[(2 * p + 1) * halves + half]
            a = a + pltpu.roll(a, 120, 1)
            b = b + pltpu.roll(b, 8, 1)
            out_ref[pl.ds((p * halves + half) * 8, 8), :] = jnp.where(even, a, b) / (
                VIEWS * 4.0 * STEPS
            )


def column_kernel(left_ref, mid_ref, right_ref, w_ref, bias_ref, wo_ref, out_ref):
    rows = mid_ref.shape[0] // 2
    blocks = rows // PD
    x = jnp.concatenate(
        [ref[pl.ds(j * rows, rows), :] for ref in (left_ref, mid_ref, right_ref) for j in range(2)],
        axis=1,
    )
    hi = x.astype(BF16)
    rest = x - hi.astype(F32)
    mid = rest.astype(BF16)
    low = (rest - mid.astype(F32)).astype(BF16)
    y3 = jnp.dot(
        jnp.concatenate([low, mid, hi], axis=0), w_ref[...], preferred_element_type=F32
    )
    y = (y3[:rows] + y3[rows : 2 * rows]) + y3[2 * rows :]
    z = y[:, :512] + bias_ref[0:1, :]
    cand = jnp.tanh(y[:, 512:] + bias_ref[1:2, :])
    small = jnp.exp(-jnp.abs(z))
    big = 1.0 / (1.0 + small)
    small = small * big
    up = z >= 0
    retain = jnp.where(up, big, small)
    fresh = jnp.where(up, small, big) * cand
    order = [(il3, p) for il3 in range(4) for p in range(PD)]

    def cut(v, il3, p):
        return v[p * blocks : (p + 1) * blocks, il3 * 128 : (il3 + 1) * 128]

    dc = None
    for il3, p in order:
        d, o = cut(retain, il3, p), cut(fresh, il3, p)
        dc, oc = (d, o) if dc is None else (d * dc, d * oc + o)
    lane = lax.broadcasted_iota(jnp.int32, (blocks, 128), 1)
    sub = lax.broadcasted_iota(jnp.int32, (blocks, 128), 0)
    first = lane < 64
    od = pltpu.roll(dc, 64, 1)
    oo = pltpu.roll(oc, 64, 1)
    pd_all = dc * od
    po_all = jnp.where(first, od * oc + oo, dc * oo + oc)
    reach = 1
    while reach < blocks:
        sd = jnp.where(sub < reach, 1.0, pltpu.roll(pd_all, reach, 0))
        so = jnp.where(sub < reach, 0.0, pltpu.roll(po_all, reach, 0))
        po_all = pd_all * so + po_all
        pd_all = pd_all * sd
        reach *= 2
    before = jnp.where(sub < 1, 0.0, pltpu.roll(po_all, 1, 0))
    h = jnp.where(first, before, od * before + oo)
    states = {}
    for il3, p in order:
        h = cut(retain, il3, p) * h + cut(fresh, il3, p)
        states[il3, p] = h
    wide = jnp.concatenate(
        [jnp.concatenate([states[il3, p] for p in range(PD)], axis=1) for il3 in range(4)], axis=0
    )
    s = jnp.dot(wide, wo_ref[...], precision=lax.Precision.HIGHEST, preferred_element_type=F32)

    def over(op, v):
        v = jnp.broadcast_to(v, (8, 128))
        v = op(v, pltpu.roll(v, 2, 1))
        v = op(v, pltpu.roll(v, 4, 1))
        return op(v, pltpu.roll(v, 8, 1))[0:1]

    row = lax.broadcasted_iota(jnp.int32, (rows, 128), 0)
    col = lax.broadcasted_iota(jnp.int32, (rows, 128), 1)
    plane = (row % blocks) * 32 + ((col // 8) % 2) * 16 + (row // blocks) * 4 + (col % 8) // 2
    value = 1.0 / (0.1 + 0.9 * plane.astype(F32) / (PD * 8 * blocks - 1))
    highest = over(jnp.maximum, jnp.max(s, axis=0, keepdims=True))
    weights = jnp.exp(s - highest)
    total = over(jnp.add, jnp.sum(weights, axis=0, keepdims=True))
    depth = over(jnp.add, jnp.sum(weights * value, axis=0, keepdims=True))
    prob = weights / total
    expected = depth / total
    for u in range(2):
        mine = prob if u == 0 else pltpu.roll(prob, 120, 1)
        message = jnp.where(col < 8, mine, expected)
        for il3 in range(4):
            out_ref[pl.ds(u * 4 + il3, blocks, stride=8), :] = message[
                il3 * blocks : (il3 + 1) * blocks
            ]


def output_kernel(x_ref, prob_ref, map_ref, ordered):
    for column, k in enumerate(path()):
        ordered[column : column + 1, :] = x_ref[k : k + 1, :]
    t = ordered[...].T
    for p in range(PD):
        prob_ref[p] = t[p * 2 : p * 2 + 2]
    map_ref[...] = t[8:10]


def gate_rows(w_gates, slab):
    w = w_gates.reshape(3, 3, 2, 32, 8).transpose(0, 1, 4, 2, 3)
    w = jnp.pad(w, ((2, 2), (0, 0), (0, 0), (0, 0), (0, 0)))
    by_row = [lax.dynamic_slice_in_dim(w, 3 - r - 2 * slab, 4, axis=0) for r in range(2)]
    v = jnp.stack(by_row, axis=4).reshape(2, 2, 3, 8, 2, 2, 32)
    v = v.transpose(4, 2, 0, 1, 3, 5, 6).reshape(2, 96, 64)
    return jnp.concatenate([v, v], axis=2)


def body(ref_feat, src_feat, tile_owner, tile_local, col_shift, w_gates, bias_z, bias_c, w_out):
    owners = lax.axis_size("depth")
    row_count, feat, cols = ref_feat.shape
    requests = tile_local.shape[0]
    tiles = src_feat.shape[0]
    blocks = owners // 8
    message = pl.pallas_call(
        message_kernel,
        out_shape=jax.ShapeDtypeStruct((owners, 128), jnp.int32),
        in_specs=[pl.BlockSpec(memory_space=pltpu.HBM)] * 3,
        out_specs=vspec(),
        scratch_shapes=[pltpu.VMEM((1, requests), jnp.int32)] * 3 + [pltpu.SemaphoreType.DMA((3,))],
        compiler_params=params(60),
        name="message",
    )(*[v.reshape(1, requests) for v in (tile_owner, tile_local, col_shift)])
    message = message.reshape(owners, 1, 128)
    asked = lax.all_to_all(message, "depth", split_axis=0, concat_axis=0, tiled=True)
    asked = asked.reshape(owners, 128)

    table, channels = pl.pallas_call(
        prepare_kernel,
        out_shape=(
            jax.ShapeDtypeStruct((row_count * (2 * MAXSHIFT + 1), feat, cols), F32),
            jax.ShapeDtypeStruct((tiles, feat, cols), BF16),
        ),
        in_specs=[vspec(), vspec()],
        out_specs=(vspec(), vspec()),
        scratch_shapes=[
            pltpu.VMEM((row_count * feat, cols), F32),
            pltpu.VMEM((tiles * feat, cols), F32),
        ],
        compiler_params=params(16),
        cost_estimate=pl.CostEstimate(flops=2000000, transcendentals=0, bytes_accessed=4000000),
        name="prepare",
    )(ref_feat, src_feat)

    def answers_of(*refs):
        answer_kernel(requests, *refs)

    answers = pl.pallas_call(
        answers_of,
        out_shape=jax.ShapeDtypeStruct((cols, blocks + blocks // 2, 128), jnp.int16),
        in_specs=[vspec(), vspec(), vspec()],
        out_specs=pl.BlockSpec(memory_space=pl.ANY),
        scratch_shapes=[
            pltpu.VMEM((cols * blocks, 128), F32),
            pltpu.VMEM((cols, blocks + blocks // 2, 128), jnp.int16),
            pltpu.VMEM((8, owners), jnp.int32),
            pltpu.SMEM((8, owners), jnp.int32),
            pltpu.SemaphoreType.DMA,
            pltpu.SemaphoreType.DMA((PIECES,)),
        ],
        compiler_params=params(10),
        name="answer",
    )(asked, table, channels)
    answers = lax.all_to_all(answers, "depth", split_axis=0, concat_axis=0, tiled=True)

    slab = lax.axis_index("slab")

    def tables_of(*refs):
        table_kernel(requests, *refs)

    targets, gates = pl.pallas_call(
        tables_of,
        out_shape=(
            jax.ShapeDtypeStruct((owners, blocks, 128), BF16),
            jax.ShapeDtypeStruct((768, 1024), BF16),
        ),
        in_specs=[vspec(), vspec()],
        out_specs=(vspec(), vspec()),
        scratch_shapes=[pltpu.VMEM((requests * blocks, 128), F32)],
        compiler_params=params(8),
        cost_estimate=pl.CostEstimate(flops=20000000, transcendentals=0, bytes_accessed=3000000),
        name="tables",
    )(asked, gate_rows(w_gates, slab))

    cost = pl.pallas_call(
        combine_kernel,
        out_shape=jax.ShapeDtypeStruct((PD * blocks, 128), F32),
        in_specs=[vspec(), vspec()],
        out_specs=vspec(),
        compiler_params=params(6),
        name="combine",
    )(answers, targets)
    both = lax.all_gather(cost, "slab", tiled=True)
    chips = path()
    pairs = list(zip(chips[:-1], chips[1:]))
    left = lax.ppermute(both, "depth", pairs)
    right = lax.ppermute(both, "depth", [(b, a) for a, b in pairs])

    bias = jnp.stack([jnp.tile(bias_z, 16), jnp.tile(bias_c, 16)])
    unit_row = jnp.arange(512, dtype=jnp.int32)[:, None] // 32
    unit_row = ((unit_row // 2) % 2) * 8 + (unit_row // 4) * 2 + unit_row % 2
    score_col = jnp.arange(128, dtype=jnp.int32)[None, :] % 16
    project = jnp.where(unit_row == score_col, jnp.tile(w_out, 16)[:, None], 0.0)
    packed = pl.pallas_call(
        column_kernel,
        out_shape=jax.ShapeDtypeStruct((owners, 128), F32),
        in_specs=[vspec()] * 6,
        out_specs=vspec(),
        compiler_params=params(10),
        name="column",
    )(left, both, right, gates, bias, project)
    packed = lax.all_to_all(
        packed.reshape(owners, 1, 128), "depth", split_axis=0, concat_axis=0, tiled=True
    )
    return pl.pallas_call(
        output_kernel,
        out_shape=(
            jax.ShapeDtypeStruct((PD, row_count, cols), F32),
            jax.ShapeDtypeStruct((row_count, cols), F32),
        ),
        in_specs=[vspec()],
        out_specs=(vspec(), vspec()),
        scratch_shapes=[pltpu.VMEM((cols, 128), F32)],
        compiler_params=params(4),
        name="output",
    )(packed.reshape(cols, 128))


def solution(mesh):
    return jax.shard_map(
        body,
        mesh=mesh,
        in_specs=(
            P("slab", None, None),
            P("depth", None, None),
            P(("depth", "slab"), None),
            P(("depth", "slab")),
            P(("depth", "slab")),
            P(),
            P(),
            P(),
            P(),
        ),
        out_specs=(P("depth", "slab", None), P("slab", None)),
        check_vma=False,
    )
```

```python
import jax
import jax.numpy as jnp
from jax import lax
from jax.experimental import pallas as pl
from jax.experimental.pallas import tpu as pltpu
from jax.sharding import PartitionSpec as P

VIEWS = 5
STEPS = 16384.0
PD = 4
MAXSHIFT = 16
F32 = jnp.float32
BF16 = jnp.bfloat16
UNROLL = 8
PIECES = 4
MIB = 1024 * 1024
TORUS = (4, 4, 8)


def params(mib):
    return pltpu.CompilerParams(vmem_limit_bytes=mib * MIB)


def column_of(k):
    nx, ny, nz = TORUS
    x, y, z = k // (ny * nz), (k // nz) % ny, k % nz
    place = x * ny + (ny - 1 - y if x % 2 else y)
    return z * nx * ny + (nx * ny - 1 - place if z % 2 else place)


def path():
    return sorted(range(TORUS[0] * TORUS[1] * TORUS[2]), key=column_of)


def message_kernel(a_ref, b_ref, c_ref, out_ref, a_s, b_s, c_s, sems):
    copies = [
        pltpu.make_async_copy(ref, scratch, sems.at[n])
        for n, (ref, scratch) in enumerate(((a_ref, a_s), (b_ref, b_s), (c_ref, c_s)))
    ]
    for copy in copies:
        copy.start()
    for copy in copies:
        copy.wait()
    rest = jnp.zeros((1, 128 - 3 * a_s.shape[1]), jnp.int32)
    row = jnp.concatenate([a_s[...], b_s[...], c_s[...], rest], axis=1)
    out_ref[...] = jnp.broadcast_to(row, out_ref.shape)


def vspec():
    return pl.BlockSpec(memory_space=pltpu.VMEM)


def sspec():
    return pl.BlockSpec(memory_space=pltpu.SMEM)


def prepare_kernel(ref_ref, src_ref, tab_ref, srce_ref, ref32, src32):
    rows, feat, cols = ref_ref.shape
    tiles = src_ref.shape[0]
    cpg = feat // 8
    for r in range(rows):
        ref32[pl.ds(r * feat, feat), :] = ref_ref[r].astype(F32)
    lane = lax.broadcasted_iota(jnp.int32, (8, cols), 1)
    for r in range(rows):
        for e in range(cpg):
            base = ref32[pl.ds(r * feat + e, 8, stride=cpg), :]
            for k in range(2 * MAXSHIFT + 1):
                shift = k - MAXSHIFT
                moved = base if shift == 0 else pltpu.roll(base, (-shift) % cols, 1)
                inside = (lane + shift >= 0) & (lane + shift < cols)
                tab_ref[r * (2 * MAXSHIFT + 1) + k, pl.ds(e * 8, 8), :] = jnp.where(inside, moved, 0.0)

    def widen(n, c):
        src32[pl.ds(n * feat, feat), :] = src_ref[n].astype(F32)
        return c

    lax.fori_loop(0, tiles, widen, 0, unroll=8)

    def reorder(n, c):
        parts = [src32[pl.ds(n * feat + e, 8, stride=cpg), :] for e in range(cpg)]
        srce_ref[n] = jnp.concatenate(parts, axis=0).astype(BF16)
        return c

    lax.fori_loop(0, tiles, reorder, 0, unroll=8)


def answer_kernel(requests, req_ref, tab_ref, srce_ref, out_ref, flat_s, coded_s, codes, table, sem, out_sem):
    owners = req_ref.shape[0]
    cols = tab_ref.shape[-1]
    blocks = owners // 8
    me = lax.axis_index("depth")
    flat = req_ref[...].T
    owner = flat[0:requests]
    local = flat[requests : 2 * requests]
    shift = flat[2 * requests : 3 * requests]
    q = lax.broadcasted_iota(jnp.int32, (requests, owners), 0)
    hit = owner == me
    first = jnp.min(jnp.where(hit, q, requests), axis=0, keepdims=True)
    last = jnp.max(jnp.where(hit, q, -1), axis=0, keepdims=True)
    value = local + (shift + MAXSHIFT) * 256 + (q % 2) * 16384
    zero = jnp.zeros_like(value)
    code0 = jnp.sum(jnp.where(hit & (q == first), value, zero), axis=0, keepdims=True)
    code1 = jnp.sum(jnp.where(hit & (q == last) & (q > first), value, zero), axis=0, keepdims=True)
    sub = lax.broadcasted_iota(jnp.int32, (8, owners), 0)
    codes[...] = jnp.where(sub == 0, code0, jnp.where(sub == 1, code1, 0))
    copy = pltpu.make_async_copy(codes, table, sem)
    copy.start()
    copy.wait()

    def one(i, s):
        code = table[s, i]
        loc = code & 255
        moved = (code >> 8) & 63
        row = code >> 14
        tile = srce_ref[loc].astype(F32) * tab_ref[row * (2 * MAXSHIFT + 1) + moved]
        total = (tile[0:8] + tile[8:16]) + (tile[16:24] + tile[24:32])
        return pltpu.roll(total, (moved + cols - MAXSHIFT) % cols, 1)

    def step(b, c):
        parts = []
        for il in range(8):
            for s in range(2):
                parts.append(one(b * 8 + il, s))
        flat_s[pl.ds(b, cols, stride=blocks), :] = jnp.concatenate(parts, axis=0).T
        return c

    lax.fori_loop(0, blocks, step, 0, unroll=UNROLL)

    size = cols // PIECES
    copies = []
    for n in range(PIECES):
        for k in range(n * size, (n + 1) * size):
            start = column_of(k) * blocks
            number = jnp.round(flat_s[start : start + blocks, :] * STEPS).astype(jnp.int32)
            low = number & 255
            coded_s[k, 0:blocks, :] = (number >> 8).astype(jnp.int16)
            pair = low[: blocks // 2] * 256 + low[blocks // 2 :] - 32768
            coded_s[k, blocks : blocks + blocks // 2, :] = pair.astype(jnp.int16)
        piece = pl.ds(n * size, size)
        copies.append(pltpu.make_async_copy(coded_s.at[piece], out_ref.at[piece], out_sem.at[n]))
        copies[-1].start()
    for copy in copies:
        copy.wait()


def table_kernel(requests, req_ref, wd_ref, target_ref, gate_ref, keys):
    owners = req_ref.shape[0]
    blocks = owners // 8
    flat = req_ref[...].T
    owner = flat[0:requests]
    q = lax.broadcasted_iota(jnp.int32, (requests, owners), 0)
    earlier = jnp.zeros((requests, owners), jnp.int32)
    for other in range(requests - 1):
        same = (owner == owner[other : other + 1]) & (q > other)
        earlier = jnp.where(same, 1, earlier)
    key = (owner * 2 + earlier).astype(F32)
    block_row = lax.broadcasted_iota(jnp.int32, (blocks, owners), 0)
    block_of = lax.broadcasted_iota(jnp.int32, (blocks, owners), 1) // 8
    own_block = block_row == block_of
    spread = []
    for n in range(requests):
        row = jnp.broadcast_to(key[n : n + 1], (blocks, owners))
        spread.append(jnp.where(own_block, row, 0.0).astype(BF16))
    inner = lax.broadcasted_iota(jnp.int32, (owners, 128), 0) % 8
    lane = lax.broadcasted_iota(jnp.int32, (owners, 128), 1)
    pick = jnp.where(inner == lane // 16, 1.0, 0.0).astype(BF16)
    wide = jnp.dot(jnp.concatenate(spread, axis=0), pick, preferred_element_type=F32)
    slot = (lax.broadcasted_iota(jnp.int32, (blocks * requests, 128), 1) // 8) % 2
    keys[...] = wide - slot.astype(F32)

    def step(n, c):
        found = [[jnp.full((8, 128), 8.0, F32) for _ in range(blocks // 8)] for _ in range(4)]
        wanted = [(2 * (n * 4 + m)).astype(F32) for m in range(4)]
        for r in range(requests):
            t = float((r // (2 * VIEWS)) * 2 + r % 2)
            for half in range(blocks // 8):
                k = keys[r * blocks + half * 8 : r * blocks + half * 8 + 8, :]
                for m in range(4):
                    found[m][half] = jnp.where(k == wanted[m], t, found[m][half])
        for m in range(4):
            target_ref[n * 4 + m] = jnp.concatenate(found[m], axis=0).astype(BF16)
        return c

    lax.fori_loop(0, owners // 4, step, 0)

    half_of = lax.broadcasted_iota(jnp.int32, (16, 128), 1) // 64
    for source in range(6):
        for zc in range(2):
            part = wd_ref[zc, source * 16 : source * 16 + 16, :]
            for il in range(8):
                mine = jnp.where(half_of == il // 4, part, jnp.zeros_like(part))
                for il3 in range(4):
                    value = mine if il3 == il % 4 else jnp.zeros_like(part)
                    gate_ref[
                        pl.ds(source * 128 + il * 16, 16), pl.ds((zc * 4 + il3) * 128, 128)
                    ] = value


def combine_kernel(ans_ref, target_ref, out_ref):
    owners = ans_ref.shape[0]
    halves = target_ref.shape[1] // 8

    def step(o, acc):
        acc = list(acc)
        targets = target_ref[o].astype(F32)
        high = ans_ref[o, 0 : halves * 8, :].astype(jnp.int32)
        pair = ans_ref[o, halves * 8 : halves * 12, :].astype(jnp.int32) + 32768
        number = high * 256 + jnp.concatenate([pair >> 8, pair & 255], axis=0)
        number = number.astype(F32)
        for half in range(halves):
            data = number[half * 8 : half * 8 + 8]
            target = targets[half * 8 : half * 8 + 8, :]
            for t in range(8):
                n = t * halves + half
                acc[n] = acc[n] + jnp.where(target == float(t), data, 0.0)
        return tuple(acc)

    zero = jnp.zeros((8, 128), F32)
    acc = lax.fori_loop(0, owners, step, (zero,) * (8 * halves), unroll=8)
    lane = lax.broadcasted_iota(jnp.int32, (8, 128), 1)
    even = (lane // 8) % 2 == 0
    for p in range(PD):
        for half in range(halves):
            a = acc[(2 * p) * halves + half]
            b = acc[(2 * p + 1) * halves + half]
            a = a + pltpu.roll(a, 120, 1)
            b = b + pltpu.roll(b, 8, 1)
            out_ref[pl.ds((p * halves + half) * 8, 8), :] = jnp.where(even, a, b) / (
                VIEWS * 4.0 * STEPS
            )


def column_kernel(first_ref, mid_ref, second_ref, w_ref, bias_ref, wo_ref, out_ref):
    rows = mid_ref.shape[0] // 2
    blocks = rows // PD
    x = jnp.concatenate(
        [ref[pl.ds(j * rows, rows), :] for ref in (first_ref, mid_ref, second_ref) for j in range(2)],
        axis=1,
    )
    hi = x.astype(BF16)
    rest = x - hi.astype(F32)
    mid = rest.astype(BF16)
    low = (rest - mid.astype(F32)).astype(BF16)
    y3 = jnp.dot(
        jnp.concatenate([low, mid, hi], axis=0), w_ref[...], preferred_element_type=F32
    )
    y = (y3[:rows] + y3[rows : 2 * rows]) + y3[2 * rows :]
    z = y[:, :512] + bias_ref[0:1, :]
    cand = jnp.tanh(y[:, 512:] + bias_ref[1:2, :])
    small = jnp.exp(-jnp.abs(z))
    big = 1.0 / (1.0 + small)
    small = small * big
    up = z >= 0
    retain = jnp.where(up, big, small)
    fresh = jnp.where(up, small, big) * cand
    order = [(il3, p) for il3 in range(4) for p in range(PD)]

    def cut(v, il3, p):
        return v[p * blocks : (p + 1) * blocks, il3 * 128 : (il3 + 1) * 128]

    dc = None
    for il3, p in order:
        d, o = cut(retain, il3, p), cut(fresh, il3, p)
        dc, oc = (d, o) if dc is None else (d * dc, d * oc + o)
    lane = lax.broadcasted_iota(jnp.int32, (blocks, 128), 1)
    sub = lax.broadcasted_iota(jnp.int32, (blocks, 128), 0)
    first = lane < 64
    od = pltpu.roll(dc, 64, 1)
    oo = pltpu.roll(oc, 64, 1)
    pd_all = dc * od
    po_all = jnp.where(first, od * oc + oo, dc * oo + oc)
    reach = 1
    while reach < blocks:
        sd = jnp.where(sub < reach, 1.0, pltpu.roll(pd_all, reach, 0))
        so = jnp.where(sub < reach, 0.0, pltpu.roll(po_all, reach, 0))
        po_all = pd_all * so + po_all
        pd_all = pd_all * sd
        reach *= 2
    before = jnp.where(sub < 1, 0.0, pltpu.roll(po_all, 1, 0))
    h = jnp.where(first, before, od * before + oo)
    states = {}
    for il3, p in order:
        h = cut(retain, il3, p) * h + cut(fresh, il3, p)
        states[il3, p] = h
    wide = jnp.concatenate(
        [jnp.concatenate([states[il3, p] for p in range(PD)], axis=1) for il3 in range(4)], axis=0
    )
    s = jnp.dot(wide, wo_ref[...], precision=lax.Precision.HIGHEST, preferred_element_type=F32)

    def over(op, v):
        v = jnp.broadcast_to(v, (8, 128))
        v = op(v, pltpu.roll(v, 2, 1))
        v = op(v, pltpu.roll(v, 4, 1))
        return op(v, pltpu.roll(v, 8, 1))[0:1]

    row = lax.broadcasted_iota(jnp.int32, (rows, 128), 0)
    col = lax.broadcasted_iota(jnp.int32, (rows, 128), 1)
    plane = (row % blocks) * 32 + ((col // 8) % 2) * 16 + (row // blocks) * 4 + (col % 8) // 2
    value = 1.0 / (0.1 + 0.9 * plane.astype(F32) / (PD * 8 * blocks - 1))
    highest = over(jnp.maximum, jnp.max(s, axis=0, keepdims=True))
    weights = jnp.exp(s - highest)
    total = over(jnp.add, jnp.sum(weights, axis=0, keepdims=True))
    depth = over(jnp.add, jnp.sum(weights * value, axis=0, keepdims=True))
    prob = weights / total
    expected = depth / total
    for u in range(2):
        mine = prob if u == 0 else pltpu.roll(prob, 120, 1)
        message = jnp.where(col < 8, mine, expected)
        for il3 in range(4):
            out_ref[pl.ds(u * 4 + il3, blocks, stride=8), :] = message[
                il3 * blocks : (il3 + 1) * blocks
            ]


def output_kernel(x_ref, prob_ref, map_ref, ordered):
    for column, k in enumerate(path()):
        ordered[column : column + 1, :] = x_ref[k : k + 1, :]
    t = ordered[...].T
    for p in range(PD):
        prob_ref[p] = t[p * 2 : p * 2 + 2]
    map_ref[...] = t[8:10]


def gate_rows(w_gates, slab, odd):
    w = w_gates.reshape(3, 3, 2, 32, 8).transpose(0, 1, 4, 2, 3)
    w = jnp.pad(w, ((2, 2), (0, 0), (0, 0), (0, 0), (0, 0)))
    by_row = [lax.dynamic_slice_in_dim(w, 3 - r - 2 * slab, 4, axis=0) for r in range(2)]
    v = jnp.stack(by_row, axis=4).reshape(2, 2, 3, 8, 2, 2, 32)
    v = jnp.where(odd, v[:, :, ::-1], v)
    v = v.transpose(4, 2, 0, 1, 3, 5, 6).reshape(2, 96, 64)
    return jnp.concatenate([v, v], axis=2)


def body(ref_feat, src_feat, tile_owner, tile_local, col_shift, w_gates, bias_z, bias_c, w_out):
    owners = lax.axis_size("depth")
    row_count, feat, cols = ref_feat.shape
    requests = tile_local.shape[0]
    tiles = src_feat.shape[0]
    blocks = owners // 8
    message = pl.pallas_call(
        message_kernel,
        out_shape=jax.ShapeDtypeStruct((owners, 128), jnp.int32),
        in_specs=[pl.BlockSpec(memory_space=pltpu.HBM)] * 3,
        out_specs=vspec(),
        scratch_shapes=[pltpu.VMEM((1, requests), jnp.int32)] * 3 + [pltpu.SemaphoreType.DMA((3,))],
        compiler_params=params(60),
        name="message",
    )(*[v.reshape(1, requests) for v in (tile_owner, tile_local, col_shift)])
    message = message.reshape(owners, 1, 128)
    asked = lax.all_to_all(message, "depth", split_axis=0, concat_axis=0, tiled=True)
    asked = asked.reshape(owners, 128)

    table, channels = pl.pallas_call(
        prepare_kernel,
        out_shape=(
            jax.ShapeDtypeStruct((row_count * (2 * MAXSHIFT + 1), feat, cols), F32),
            jax.ShapeDtypeStruct((tiles, feat, cols), BF16),
        ),
        in_specs=[vspec(), vspec()],
        out_specs=(vspec(), vspec()),
        scratch_shapes=[
            pltpu.VMEM((row_count * feat, cols), F32),
            pltpu.VMEM((tiles * feat, cols), F32),
        ],
        compiler_params=params(16),
        cost_estimate=pl.CostEstimate(flops=2000000, transcendentals=0, bytes_accessed=4000000),
        name="prepare",
    )(ref_feat, src_feat)

    def answers_of(*refs):
        answer_kernel(requests, *refs)

    answers = pl.pallas_call(
        answers_of,
        out_shape=jax.ShapeDtypeStruct((cols, blocks + blocks // 2, 128), jnp.int16),
        in_specs=[vspec(), vspec(), vspec()],
        out_specs=pl.BlockSpec(memory_space=pl.ANY),
        scratch_shapes=[
            pltpu.VMEM((cols * blocks, 128), F32),
            pltpu.VMEM((cols, blocks + blocks // 2, 128), jnp.int16),
            pltpu.VMEM((8, owners), jnp.int32),
            pltpu.SMEM((8, owners), jnp.int32),
            pltpu.SemaphoreType.DMA,
            pltpu.SemaphoreType.DMA((PIECES,)),
        ],
        compiler_params=params(10),
        name="answer",
    )(asked, table, channels)
    answers = lax.all_to_all(answers, "depth", split_axis=0, concat_axis=0, tiled=True)

    slab = lax.axis_index("slab")
    depth = lax.axis_index("depth")
    odd = (depth // (TORUS[1] * TORUS[2]) + depth // TORUS[2] + depth) % 2 == 1

    def tables_of(*refs):
        table_kernel(requests, *refs)

    targets, gates = pl.pallas_call(
        tables_of,
        out_shape=(
            jax.ShapeDtypeStruct((owners, blocks, 128), BF16),
            jax.ShapeDtypeStruct((768, 1024), BF16),
        ),
        in_specs=[vspec(), vspec()],
        out_specs=(vspec(), vspec()),
        scratch_shapes=[pltpu.VMEM((requests * blocks, 128), F32)],
        compiler_params=params(8),
        cost_estimate=pl.CostEstimate(flops=20000000, transcendentals=0, bytes_accessed=3000000),
        name="tables",
    )(asked, gate_rows(w_gates, slab, odd))

    cost = pl.pallas_call(
        combine_kernel,
        out_shape=jax.ShapeDtypeStruct((PD * blocks, 128), F32),
        in_specs=[vspec(), vspec()],
        out_specs=vspec(),
        compiler_params=params(6),
        name="combine",
    )(answers, targets)
    both = lax.all_gather(cost, "slab", tiled=True)
    chips = path()

    def exchange(start):
        pairs = [(chips[i], chips[i + 1]) for i in range(start, owners - 1, 2)]
        return lax.ppermute(both, "depth", pairs + [(b, a) for a, b in pairs])

    first, second = exchange(1), exchange(0)

    bias = jnp.stack([jnp.tile(bias_z, 16), jnp.tile(bias_c, 16)])
    unit_row = jnp.arange(512, dtype=jnp.int32)[:, None] // 32
    unit_row = ((unit_row // 2) % 2) * 8 + (unit_row // 4) * 2 + unit_row % 2
    score_col = jnp.arange(128, dtype=jnp.int32)[None, :] % 16
    project = jnp.where(unit_row == score_col, jnp.tile(w_out, 16)[:, None], 0.0)
    packed = pl.pallas_call(
        column_kernel,
        out_shape=jax.ShapeDtypeStruct((owners, 128), F32),
        in_specs=[vspec()] * 6,
        out_specs=vspec(),
        compiler_params=params(10),
        name="column",
    )(first, both, second, gates, bias, project)
    packed = lax.all_to_all(
        packed.reshape(owners, 1, 128), "depth", split_axis=0, concat_axis=0, tiled=True
    )
    return pl.pallas_call(
        output_kernel,
        out_shape=(
            jax.ShapeDtypeStruct((PD, row_count, cols), F32),
            jax.ShapeDtypeStruct((row_count, cols), F32),
        ),
        in_specs=[vspec()],
        out_specs=(vspec(), vspec()),
        scratch_shapes=[pltpu.VMEM((cols, 128), F32)],
        compiler_params=params(4),
        name="output",
    )(packed.reshape(cols, 128))


def solution(mesh):
    return jax.shard_map(
        body,
        mesh=mesh,
        in_specs=(
            P("slab", None, None),
            P("depth", None, None),
            P(("depth", "slab"), None),
            P(("depth", "slab")),
            P(("depth", "slab")),
            P(),
            P(),
            P(),
            P(),
        ),
        out_specs=(P("depth", "slab", None), P("slab", None)),
        check_vma=False,
    )
```

```python
import jax
import jax.numpy as jnp
from jax import lax
from jax.experimental import pallas as pl
from jax.experimental.pallas import tpu as pltpu
from jax.sharding import PartitionSpec as P

VIEWS = 5
STEPS = 1618.0
PD = 4
MAXSHIFT = 16
F32 = jnp.float32
BF16 = jnp.bfloat16
UNROLL = 8
PIECES = 4
WORDS = 10
MIB = 1024 * 1024
TORUS = (4, 4, 8)


def params(mib):
    return pltpu.CompilerParams(vmem_limit_bytes=mib * MIB)


def column_of(k):
    nx, ny, nz = TORUS
    x, y, z = k // (ny * nz), (k // nz) % ny, k % nz
    place = x * ny + (ny - 1 - y if x % 2 else y)
    return z * nx * ny + (nx * ny - 1 - place if z % 2 else place)


def path():
    return sorted(range(TORUS[0] * TORUS[1] * TORUS[2]), key=column_of)


def message_kernel(a_ref, b_ref, c_ref, out_ref, a_s, b_s, c_s, sems):
    copies = [
        pltpu.make_async_copy(ref, scratch, sems.at[n])
        for n, (ref, scratch) in enumerate(((a_ref, a_s), (b_ref, b_s), (c_ref, c_s)))
    ]
    for copy in copies:
        copy.start()
    for copy in copies:
        copy.wait()
    rest = jnp.zeros((1, 128 - 3 * a_s.shape[1]), jnp.int32)
    row = jnp.concatenate([a_s[...], b_s[...], c_s[...], rest], axis=1)
    out_ref[...] = jnp.broadcast_to(row, out_ref.shape)


def vspec():
    return pl.BlockSpec(memory_space=pltpu.VMEM)


def sspec():
    return pl.BlockSpec(memory_space=pltpu.SMEM)


def prepare_kernel(ref_ref, src_ref, tab_ref, srce_ref, ref32, src32):
    rows, feat, cols = ref_ref.shape
    tiles = src_ref.shape[0]
    cpg = feat // 8
    for r in range(rows):
        ref32[pl.ds(r * feat, feat), :] = ref_ref[r].astype(F32)
    lane = lax.broadcasted_iota(jnp.int32, (8, cols), 1)
    for r in range(rows):
        for e in range(cpg):
            base = ref32[pl.ds(r * feat + e, 8, stride=cpg), :]
            for k in range(2 * MAXSHIFT + 1):
                shift = k - MAXSHIFT
                moved = base if shift == 0 else pltpu.roll(base, (-shift) % cols, 1)
                inside = (lane + shift >= 0) & (lane + shift < cols)
                tab_ref[r * (2 * MAXSHIFT + 1) + k, pl.ds(e * 8, 8), :] = jnp.where(inside, moved, 0.0)

    def widen(n, c):
        src32[pl.ds(n * feat, feat), :] = src_ref[n].astype(F32)
        return c

    lax.fori_loop(0, tiles, widen, 0, unroll=8)

    def reorder(n, c):
        parts = [src32[pl.ds(n * feat + e, 8, stride=cpg), :] for e in range(cpg)]
        srce_ref[n] = jnp.concatenate(parts, axis=0).astype(BF16)
        return c

    lax.fori_loop(0, tiles, reorder, 0, unroll=8)


def answer_kernel(requests, req_ref, tab_ref, srce_ref, out_ref, flat_s, coded_s, codes, table, sem, out_sem):
    owners = req_ref.shape[0]
    cols = tab_ref.shape[-1]
    blocks = owners // 8
    me = lax.axis_index("depth")
    flat = req_ref[...].T
    owner = flat[0:requests]
    local = flat[requests : 2 * requests]
    shift = flat[2 * requests : 3 * requests]
    q = lax.broadcasted_iota(jnp.int32, (requests, owners), 0)
    hit = owner == me
    first = jnp.min(jnp.where(hit, q, requests), axis=0, keepdims=True)
    last = jnp.max(jnp.where(hit, q, -1), axis=0, keepdims=True)
    value = local + (shift + MAXSHIFT) * 256 + (q % 2) * 16384
    zero = jnp.zeros_like(value)
    code0 = jnp.sum(jnp.where(hit & (q == first), value, zero), axis=0, keepdims=True)
    code1 = jnp.sum(jnp.where(hit & (q == last) & (q > first), value, zero), axis=0, keepdims=True)
    sub = lax.broadcasted_iota(jnp.int32, (8, owners), 0)
    codes[...] = jnp.where(sub == 0, code0, jnp.where(sub == 1, code1, 0))
    copy = pltpu.make_async_copy(codes, table, sem)
    copy.start()
    copy.wait()

    def one(i, s):
        code = table[s, i]
        loc = code & 255
        moved = (code >> 8) & 63
        row = code >> 14
        tile = srce_ref[loc].astype(F32) * tab_ref[row * (2 * MAXSHIFT + 1) + moved]
        total = (tile[0:8] + tile[8:16]) + (tile[16:24] + tile[24:32])
        return pltpu.roll(total, (moved + cols - MAXSHIFT) % cols, 1)

    def step(b, c):
        parts = []
        for il in range(8):
            for s in range(2):
                parts.append(one(b * 8 + il, s))
        flat_s[pl.ds(b, cols, stride=blocks), :] = jnp.concatenate(parts, axis=0).T
        return c

    lax.fori_loop(0, blocks, step, 0, unroll=UNROLL)

    half = blocks // 2
    place = lax.broadcasted_iota(jnp.int32, (half, cols), 0) * 4
    size = cols // PIECES
    copies = []
    for n in range(PIECES):
        for k in range(n * size, (n + 1) * size):
            start = column_of(k) * blocks
            number = jnp.round(flat_s[start : start + blocks, :] * STEPS).astype(jnp.int32)
            high = number >> 4
            low = number & 15
            at = k * WORDS
            coded_s[at : at + half, :] = (high[:half] << 16) | (high[half:] & 65535)
            coded_s[at + half : at + half + 1, :] = jnp.sum(
                low[:half] << place, axis=0, keepdims=True
            )
            coded_s[at + half + 1 : at + WORDS, :] = jnp.sum(
                low[half:] << place, axis=0, keepdims=True
            )
        piece = pl.ds(n * size * WORDS, size * WORDS)
        copies.append(pltpu.make_async_copy(coded_s.at[piece], out_ref.at[piece], out_sem.at[n]))
        copies[-1].start()
    for copy in copies:
        copy.wait()


def table_kernel(requests, req_ref, wd_ref, target_ref, gate_ref, keys):
    owners = req_ref.shape[0]
    blocks = owners // 8
    flat = req_ref[...].T
    owner = flat[0:requests]
    q = lax.broadcasted_iota(jnp.int32, (requests, owners), 0)
    earlier = jnp.zeros((requests, owners), jnp.int32)
    for other in range(requests - 1):
        same = (owner == owner[other : other + 1]) & (q > other)
        earlier = jnp.where(same, 1, earlier)
    key = (owner * 2 + earlier).astype(F32)
    block_row = lax.broadcasted_iota(jnp.int32, (blocks, owners), 0)
    block_of = lax.broadcasted_iota(jnp.int32, (blocks, owners), 1) // 8
    own_block = block_row == block_of
    spread = []
    for n in range(requests):
        row = jnp.broadcast_to(key[n : n + 1], (blocks, owners))
        spread.append(jnp.where(own_block, row, 0.0).astype(BF16))
    inner = lax.broadcasted_iota(jnp.int32, (owners, 128), 0) % 8
    lane = lax.broadcasted_iota(jnp.int32, (owners, 128), 1)
    pick = jnp.where(inner == lane // 16, 1.0, 0.0).astype(BF16)
    wide = jnp.dot(jnp.concatenate(spread, axis=0), pick, preferred_element_type=F32)
    slot = (lax.broadcasted_iota(jnp.int32, (blocks * requests, 128), 1) // 8) % 2
    keys[...] = wide - slot.astype(F32)

    def step(n, c):
        found = [[jnp.full((8, 128), 8.0, F32) for _ in range(blocks // 8)] for _ in range(4)]
        wanted = [(2 * (n * 4 + m)).astype(F32) for m in range(4)]
        for r in range(requests):
            t = float((r // (2 * VIEWS)) * 2 + r % 2)
            for half in range(blocks // 8):
                k = keys[r * blocks + half * 8 : r * blocks + half * 8 + 8, :]
                for m in range(4):
                    found[m][half] = jnp.where(k == wanted[m], t, found[m][half])
        for m in range(4):
            target_ref[n * 4 + m] = jnp.concatenate(found[m], axis=0).astype(BF16)
        return c

    lax.fori_loop(0, owners // 4, step, 0)

    half_of = lax.broadcasted_iota(jnp.int32, (16, 128), 1) // 64
    for source in range(6):
        for zc in range(2):
            part = wd_ref[zc, source * 16 : source * 16 + 16, :]
            for il in range(8):
                mine = jnp.where(half_of == il // 4, part, jnp.zeros_like(part))
                for il3 in range(4):
                    value = mine if il3 == il % 4 else jnp.zeros_like(part)
                    gate_ref[
                        pl.ds(source * 128 + il * 16, 16), pl.ds((zc * 4 + il3) * 128, 128)
                    ] = value


def combine_kernel(ans_ref, target_ref, out_ref):
    owners = target_ref.shape[0]
    halves = target_ref.shape[1] // 8
    place = lax.broadcasted_iota(jnp.int32, (8, 128), 0) * 4

    def step(n, acc):
        acc = list(acc)
        start = pl.multiple_of(n * 4 * WORDS, 8)
        words = ans_ref[pl.ds(start, 4 * WORDS), :]
        for m in range(4):
            mine = words[m * WORDS : (m + 1) * WORDS]
            targets = target_ref[n * 4 + m].astype(F32)
            high = (mine[:8] >> 16, (mine[:8] << 16) >> 16)
            for half in range(halves):
                low = (jnp.broadcast_to(mine[8 + half : 9 + half], (8, 128)) >> place) & 15
                data = (high[half] * 16 + low).astype(F32)
                target = targets[half * 8 : half * 8 + 8, :]
                for t in range(8):
                    i = t * halves + half
                    acc[i] = acc[i] + jnp.where(target == float(t), data, 0.0)
        return tuple(acc)

    zero = jnp.zeros((8, 128), F32)
    acc = lax.fori_loop(0, owners // 4, step, (zero,) * (8 * halves), unroll=2)
    lane = lax.broadcasted_iota(jnp.int32, (8, 128), 1)
    even = (lane // 8) % 2 == 0
    for p in range(PD):
        for half in range(halves):
            a = acc[(2 * p) * halves + half]
            b = acc[(2 * p + 1) * halves + half]
            a = a + pltpu.roll(a, 120, 1)
            b = b + pltpu.roll(b, 8, 1)
            out_ref[pl.ds((p * halves + half) * 8, 8), :] = jnp.where(even, a, b) / (
                VIEWS * 4.0 * STEPS
            )


def column_kernel(first_ref, mid_ref, second_ref, w_ref, bias_ref, wo_ref, out_ref):
    rows = mid_ref.shape[0] // 2
    blocks = rows // PD
    x = jnp.concatenate(
        [ref[pl.ds(j * rows, rows), :] for ref in (first_ref, mid_ref, second_ref) for j in range(2)],
        axis=1,
    )
    hi = x.astype(BF16)
    rest = x - hi.astype(F32)
    mid = rest.astype(BF16)
    low = (rest - mid.astype(F32)).astype(BF16)
    y3 = jnp.dot(
        jnp.concatenate([low, mid, hi], axis=0), w_ref[...], preferred_element_type=F32
    )
    y = (y3[:rows] + y3[rows : 2 * rows]) + y3[2 * rows :]
    z = y[:, :512] + bias_ref[0:1, :]
    cand = jnp.tanh(y[:, 512:] + bias_ref[1:2, :])
    small = jnp.exp(-jnp.abs(z))
    big = 1.0 / (1.0 + small)
    small = small * big
    up = z >= 0
    retain = jnp.where(up, big, small)
    fresh = jnp.where(up, small, big) * cand
    order = [(il3, p) for il3 in range(4) for p in range(PD)]

    def cut(v, il3, p):
        return v[p * blocks : (p + 1) * blocks, il3 * 128 : (il3 + 1) * 128]

    dc = None
    for il3, p in order:
        d, o = cut(retain, il3, p), cut(fresh, il3, p)
        dc, oc = (d, o) if dc is None else (d * dc, d * oc + o)
    lane = lax.broadcasted_iota(jnp.int32, (blocks, 128), 1)
    sub = lax.broadcasted_iota(jnp.int32, (blocks, 128), 0)
    first = lane < 64
    od = pltpu.roll(dc, 64, 1)
    oo = pltpu.roll(oc, 64, 1)
    pd_all = dc * od
    po_all = jnp.where(first, od * oc + oo, dc * oo + oc)
    reach = 1
    while reach < blocks:
        sd = jnp.where(sub < reach, 1.0, pltpu.roll(pd_all, reach, 0))
        so = jnp.where(sub < reach, 0.0, pltpu.roll(po_all, reach, 0))
        po_all = pd_all * so + po_all
        pd_all = pd_all * sd
        reach *= 2
    before = jnp.where(sub < 1, 0.0, pltpu.roll(po_all, 1, 0))
    h = jnp.where(first, before, od * before + oo)
    states = {}
    for il3, p in order:
        h = cut(retain, il3, p) * h + cut(fresh, il3, p)
        states[il3, p] = h
    wide = jnp.concatenate(
        [jnp.concatenate([states[il3, p] for p in range(PD)], axis=1) for il3 in range(4)], axis=0
    )
    s = jnp.dot(wide, wo_ref[...], precision=lax.Precision.HIGHEST, preferred_element_type=F32)

    def over(op, v):
        v = jnp.broadcast_to(v, (8, 128))
        v = op(v, pltpu.roll(v, 2, 1))
        v = op(v, pltpu.roll(v, 4, 1))
        return op(v, pltpu.roll(v, 8, 1))[0:1]

    row = lax.broadcasted_iota(jnp.int32, (rows, 128), 0)
    col = lax.broadcasted_iota(jnp.int32, (rows, 128), 1)
    plane = (row % blocks) * 32 + ((col // 8) % 2) * 16 + (row // blocks) * 4 + (col % 8) // 2
    value = 1.0 / (0.1 + 0.9 * plane.astype(F32) / (PD * 8 * blocks - 1))
    highest = over(jnp.maximum, jnp.max(s, axis=0, keepdims=True))
    weights = jnp.exp(s - highest)
    total = over(jnp.add, jnp.sum(weights, axis=0, keepdims=True))
    depth = over(jnp.add, jnp.sum(weights * value, axis=0, keepdims=True))
    prob = weights / total
    expected = depth / total
    for u in range(2):
        mine = prob if u == 0 else pltpu.roll(prob, 120, 1)
        message = jnp.where(col < 8, mine, expected)
        for il3 in range(4):
            out_ref[pl.ds(u * 4 + il3, blocks, stride=8), :] = message[
                il3 * blocks : (il3 + 1) * blocks
            ]


def output_kernel(x_ref, prob_ref, map_ref, ordered):
    for column, k in enumerate(path()):
        ordered[column : column + 1, :] = x_ref[k : k + 1, :]
    t = ordered[...].T
    for p in range(PD):
        prob_ref[p] = t[p * 2 : p * 2 + 2]
    map_ref[...] = t[8:10]


def gate_rows(w_gates, slab, odd):
    w = w_gates.reshape(3, 3, 2, 32, 8).transpose(0, 1, 4, 2, 3)
    w = jnp.pad(w, ((2, 2), (0, 0), (0, 0), (0, 0), (0, 0)))
    by_row = [lax.dynamic_slice_in_dim(w, 3 - r - 2 * slab, 4, axis=0) for r in range(2)]
    v = jnp.stack(by_row, axis=4).reshape(2, 2, 3, 8, 2, 2, 32)
    v = jnp.where(odd, v[:, :, ::-1], v)
    v = v.transpose(4, 2, 0, 1, 3, 5, 6).reshape(2, 96, 64)
    return jnp.concatenate([v, v], axis=2)


def body(ref_feat, src_feat, tile_owner, tile_local, col_shift, w_gates, bias_z, bias_c, w_out):
    owners = lax.axis_size("depth")
    row_count, feat, cols = ref_feat.shape
    requests = tile_local.shape[0]
    tiles = src_feat.shape[0]
    blocks = owners // 8
    message = pl.pallas_call(
        message_kernel,
        out_shape=jax.ShapeDtypeStruct((owners, 128), jnp.int32),
        in_specs=[pl.BlockSpec(memory_space=pltpu.HBM)] * 3,
        out_specs=vspec(),
        scratch_shapes=[pltpu.VMEM((1, requests), jnp.int32)] * 3 + [pltpu.SemaphoreType.DMA((3,))],
        compiler_params=params(60),
        name="message",
    )(*[v.reshape(1, requests) for v in (tile_owner, tile_local, col_shift)])
    message = message.reshape(owners, 1, 128)
    asked = lax.all_to_all(message, "depth", split_axis=0, concat_axis=0, tiled=True)
    asked = asked.reshape(owners, 128)

    table, channels = pl.pallas_call(
        prepare_kernel,
        out_shape=(
            jax.ShapeDtypeStruct((row_count * (2 * MAXSHIFT + 1), feat, cols), F32),
            jax.ShapeDtypeStruct((tiles, feat, cols), BF16),
        ),
        in_specs=[vspec(), vspec()],
        out_specs=(vspec(), vspec()),
        scratch_shapes=[
            pltpu.VMEM((row_count * feat, cols), F32),
            pltpu.VMEM((tiles * feat, cols), F32),
        ],
        compiler_params=params(16),
        cost_estimate=pl.CostEstimate(flops=2000000, transcendentals=0, bytes_accessed=4000000),
        name="prepare",
    )(ref_feat, src_feat)

    def answers_of(*refs):
        answer_kernel(requests, *refs)

    answers = pl.pallas_call(
        answers_of,
        out_shape=jax.ShapeDtypeStruct((cols * WORDS, 128), jnp.int32),
        in_specs=[vspec(), vspec(), vspec()],
        out_specs=pl.BlockSpec(memory_space=pl.ANY),
        scratch_shapes=[
            pltpu.VMEM((cols * blocks, 128), F32),
            pltpu.VMEM((cols * WORDS, 128), jnp.int32),
            pltpu.VMEM((8, owners), jnp.int32),
            pltpu.SMEM((8, owners), jnp.int32),
            pltpu.SemaphoreType.DMA,
            pltpu.SemaphoreType.DMA((PIECES,)),
        ],
        compiler_params=params(10),
        name="answer",
    )(asked, table, channels)
    answers = lax.all_to_all(
        answers.reshape(cols, 1, WORDS * 128), "depth", split_axis=0, concat_axis=0, tiled=True
    )

    slab = lax.axis_index("slab")
    depth = lax.axis_index("depth")
    odd = (depth // (TORUS[1] * TORUS[2]) + depth // TORUS[2] + depth) % 2 == 1

    def tables_of(*refs):
        table_kernel(requests, *refs)

    targets, gates = pl.pallas_call(
        tables_of,
        out_shape=(
            jax.ShapeDtypeStruct((owners, blocks, 128), BF16),
            jax.ShapeDtypeStruct((768, 1024), BF16),
        ),
        in_specs=[vspec(), vspec()],
        out_specs=(vspec(), vspec()),
        scratch_shapes=[pltpu.VMEM((requests * blocks, 128), F32)],
        compiler_params=params(8),
        cost_estimate=pl.CostEstimate(flops=20000000, transcendentals=0, bytes_accessed=3000000),
        name="tables",
    )(asked, gate_rows(w_gates, slab, odd))

    cost = pl.pallas_call(
        combine_kernel,
        out_shape=jax.ShapeDtypeStruct((PD * blocks, 128), F32),
        in_specs=[vspec(), vspec()],
        out_specs=vspec(),
        compiler_params=params(6),
        name="combine",
    )(answers.reshape(owners * WORDS, 128), targets)
    both = lax.all_gather(cost, "slab", tiled=True)
    chips = path()

    def exchange(start):
        pairs = [(chips[i], chips[i + 1]) for i in range(start, owners - 1, 2)]
        return lax.ppermute(both, "depth", pairs + [(b, a) for a, b in pairs])

    first, second = exchange(1), exchange(0)

    bias = jnp.stack([jnp.tile(bias_z, 16), jnp.tile(bias_c, 16)])
    unit_row = jnp.arange(512, dtype=jnp.int32)[:, None] // 32
    unit_row = ((unit_row // 2) % 2) * 8 + (unit_row // 4) * 2 + unit_row % 2
    score_col = jnp.arange(128, dtype=jnp.int32)[None, :] % 16
    project = jnp.where(unit_row == score_col, jnp.tile(w_out, 16)[:, None], 0.0)
    packed = pl.pallas_call(
        column_kernel,
        out_shape=jax.ShapeDtypeStruct((owners, 128), F32),
        in_specs=[vspec()] * 6,
        out_specs=vspec(),
        compiler_params=params(10),
        name="column",
    )(first, both, second, gates, bias, project)
    packed = lax.all_to_all(
        packed.reshape(owners, 1, 128), "depth", split_axis=0, concat_axis=0, tiled=True
    )
    return pl.pallas_call(
        output_kernel,
        out_shape=(
            jax.ShapeDtypeStruct((PD, row_count, cols), F32),
            jax.ShapeDtypeStruct((row_count, cols), F32),
        ),
        in_specs=[vspec()],
        out_specs=(vspec(), vspec()),
        scratch_shapes=[pltpu.VMEM((cols, 128), F32)],
        compiler_params=params(4),
        name="output",
    )(packed.reshape(cols, 128))


def solution(mesh):
    return jax.shard_map(
        body,
        mesh=mesh,
        in_specs=(
            P("slab", None, None),
            P("depth", None, None),
            P(("depth", "slab"), None),
            P(("depth", "slab")),
            P(("depth", "slab")),
            P(),
            P(),
            P(),
            P(),
        ),
        out_specs=(P("depth", "slab", None), P("slab", None)),
        check_vma=False,
    )
```

```python
import jax
import jax.numpy as jnp
from jax import lax
from jax.experimental import pallas as pl
from jax.experimental.pallas import tpu as pltpu
from jax.sharding import PartitionSpec as P

VIEWS = 5
STEPS = 1618.0
PD = 4
MAXSHIFT = 16
F32 = jnp.float32
BF16 = jnp.bfloat16
UNROLL = 16
PIECES = 8
WORDS = 10
MIB = 1024 * 1024
TORUS = (4, 4, 8)


def params(mib):
    return pltpu.CompilerParams(vmem_limit_bytes=mib * MIB)


def column_of(k):
    nx, ny, nz = TORUS
    x, y, z = k // (ny * nz), (k // nz) % ny, k % nz
    place = x * ny + (ny - 1 - y if x % 2 else y)
    return z * nx * ny + (nx * ny - 1 - place if z % 2 else place)


def path():
    return sorted(range(TORUS[0] * TORUS[1] * TORUS[2]), key=column_of)


def message_kernel(a_ref, b_ref, c_ref, out_ref, a_s, b_s, c_s, sems):
    copies = [
        pltpu.make_async_copy(ref, scratch, sems.at[n])
        for n, (ref, scratch) in enumerate(((a_ref, a_s), (b_ref, b_s), (c_ref, c_s)))
    ]
    for copy in copies:
        copy.start()
    for copy in copies:
        copy.wait()
    rest = jnp.zeros((1, 128 - 3 * a_s.shape[1]), jnp.int32)
    row = jnp.concatenate([a_s[...], b_s[...], c_s[...], rest], axis=1)
    out_ref[...] = jnp.broadcast_to(row, out_ref.shape)


def vspec():
    return pl.BlockSpec(memory_space=pltpu.VMEM)


def sspec():
    return pl.BlockSpec(memory_space=pltpu.SMEM)


def prepare_kernel(ref_ref, src_ref, tab_ref, srce_ref, ref32, src32):
    rows, feat, cols = ref_ref.shape
    tiles = src_ref.shape[0]
    cpg = feat // 8
    for r in range(rows):
        ref32[pl.ds(r * feat, feat), :] = ref_ref[r].astype(F32)
    lane = lax.broadcasted_iota(jnp.int32, (8, cols), 1)
    for r in range(rows):
        for e in range(cpg):
            base = ref32[pl.ds(r * feat + e, 8, stride=cpg), :]
            for k in range(2 * MAXSHIFT + 1):
                shift = k - MAXSHIFT
                moved = base if shift == 0 else pltpu.roll(base, (-shift) % cols, 1)
                inside = (lane + shift >= 0) & (lane + shift < cols)
                tab_ref[r * (2 * MAXSHIFT + 1) + k, pl.ds(e * 8, 8), :] = jnp.where(inside, moved, 0.0)

    def widen(n, c):
        src32[pl.ds(n * feat, feat), :] = src_ref[n].astype(F32)
        return c

    lax.fori_loop(0, tiles, widen, 0, unroll=8)

    def reorder(n, c):
        parts = [src32[pl.ds(n * feat + e, 8, stride=cpg), :] for e in range(cpg)]
        srce_ref[n] = jnp.concatenate(parts, axis=0).astype(BF16)
        return c

    lax.fori_loop(0, tiles, reorder, 0, unroll=8)


def answer_kernel(requests, req_ref, tab_ref, srce_ref, out_ref, flat_s, coded_s, codes, table, sem, out_sem):
    owners = req_ref.shape[0]
    cols = tab_ref.shape[-1]
    blocks = owners // 8
    me = lax.axis_index("depth")
    flat = req_ref[...].T
    owner = flat[0:requests]
    local = flat[requests : 2 * requests]
    shift = flat[2 * requests : 3 * requests]
    q = lax.broadcasted_iota(jnp.int32, (requests, owners), 0)
    hit = owner == me
    first = jnp.min(jnp.where(hit, q, requests), axis=0, keepdims=True)
    last = jnp.max(jnp.where(hit, q, -1), axis=0, keepdims=True)
    value = local + (shift + MAXSHIFT) * 256 + (q % 2) * 16384
    zero = jnp.zeros_like(value)
    code0 = jnp.sum(jnp.where(hit & (q == first), value, zero), axis=0, keepdims=True)
    code1 = jnp.sum(jnp.where(hit & (q == last) & (q > first), value, zero), axis=0, keepdims=True)
    sub = lax.broadcasted_iota(jnp.int32, (8, owners), 0)
    codes[...] = jnp.where(sub == 0, code0, jnp.where(sub == 1, code1, 0))
    copy = pltpu.make_async_copy(codes, table, sem)
    copy.start()
    copy.wait()

    def one(i, s):
        code = table[s, i]
        loc = code & 255
        moved = (code >> 8) & 63
        row = code >> 14
        tile = srce_ref[loc].astype(F32) * tab_ref[row * (2 * MAXSHIFT + 1) + moved]
        total = (tile[0:8] + tile[8:16]) + (tile[16:24] + tile[24:32])
        return pltpu.roll(total, (moved + cols - MAXSHIFT) % cols, 1)

    def step(b, c):
        parts = []
        for il in range(8):
            for s in range(2):
                parts.append(one(b * 8 + il, s))
        flat_s[pl.ds(b, cols, stride=blocks), :] = jnp.concatenate(parts, axis=0).T
        return c

    lax.fori_loop(0, blocks, step, 0, unroll=UNROLL)

    half = blocks // 2
    place = lax.broadcasted_iota(jnp.int32, (half, cols), 0) * 4
    size = cols // PIECES
    copies = []
    for n in range(PIECES):
        for k in range(n * size, (n + 1) * size):
            start = column_of(k) * blocks
            number = jnp.round(flat_s[start : start + blocks, :] * STEPS).astype(jnp.int32)
            high = number >> 4
            low = number & 15
            at = k * WORDS
            coded_s[at : at + half, :] = (high[:half] << 16) | (high[half:] & 65535)
            coded_s[at + half : at + half + 1, :] = jnp.sum(
                low[:half] << place, axis=0, keepdims=True
            )
            coded_s[at + half + 1 : at + WORDS, :] = jnp.sum(
                low[half:] << place, axis=0, keepdims=True
            )
        piece = pl.ds(n * size * WORDS, size * WORDS)
        copies.append(pltpu.make_async_copy(coded_s.at[piece], out_ref.at[piece], out_sem.at[n]))
        copies[-1].start()
    for copy in copies:
        copy.wait()


def table_kernel(requests, req_ref, wd_ref, target_ref, gate_ref, keys):
    owners = req_ref.shape[0]
    blocks = owners // 8
    flat = req_ref[...].T
    owner = flat[0:requests]
    q = lax.broadcasted_iota(jnp.int32, (requests, owners), 0)
    earlier = jnp.zeros((requests, owners), jnp.int32)
    for other in range(requests - 1):
        same = (owner == owner[other : other + 1]) & (q > other)
        earlier = jnp.where(same, 1, earlier)
    key = (owner * 2 + earlier).astype(F32)
    block_row = lax.broadcasted_iota(jnp.int32, (blocks, owners), 0)
    block_of = lax.broadcasted_iota(jnp.int32, (blocks, owners), 1) // 8
    own_block = block_row == block_of
    spread = []
    for n in range(requests):
        row = jnp.broadcast_to(key[n : n + 1], (blocks, owners))
        spread.append(jnp.where(own_block, row, 0.0).astype(BF16))
    inner = lax.broadcasted_iota(jnp.int32, (owners, 128), 0) % 8
    lane = lax.broadcasted_iota(jnp.int32, (owners, 128), 1)
    pick = jnp.where(inner == lane // 16, 1.0, 0.0).astype(BF16)
    wide = jnp.dot(jnp.concatenate(spread, axis=0), pick, preferred_element_type=F32)
    slot = (lax.broadcasted_iota(jnp.int32, (blocks * requests, 128), 1) // 8) % 2
    keys[...] = wide - slot.astype(F32)

    def step(n, c):
        found = [[jnp.full((8, 128), 8.0, F32) for _ in range(blocks // 8)] for _ in range(4)]
        wanted = [(2 * (n * 4 + m)).astype(F32) for m in range(4)]
        for r in range(requests):
            t = float((r // (2 * VIEWS)) * 2 + r % 2)
            for half in range(blocks // 8):
                k = keys[r * blocks + half * 8 : r * blocks + half * 8 + 8, :]
                for m in range(4):
                    found[m][half] = jnp.where(k == wanted[m], t, found[m][half])
        for m in range(4):
            target_ref[n * 4 + m] = jnp.concatenate(found[m], axis=0).astype(BF16)
        return c

    lax.fori_loop(0, owners // 4, step, 0)

    half_of = lax.broadcasted_iota(jnp.int32, (16, 128), 1) // 64
    for source in range(6):
        for zc in range(2):
            part = wd_ref[zc, source * 16 : source * 16 + 16, :]
            for il in range(8):
                mine = jnp.where(half_of == il // 4, part, jnp.zeros_like(part))
                for il3 in range(4):
                    value = mine if il3 == il % 4 else jnp.zeros_like(part)
                    gate_ref[
                        pl.ds(source * 128 + il * 16, 16), pl.ds((zc * 4 + il3) * 128, 128)
                    ] = value


def combine_kernel(ans_ref, target_ref, out_ref):
    owners = target_ref.shape[0]
    halves = target_ref.shape[1] // 8
    place = lax.broadcasted_iota(jnp.int32, (8, 128), 0) * 4

    def step(n, acc):
        acc = list(acc)
        start = pl.multiple_of(n * 4 * WORDS, 8)
        words = ans_ref[pl.ds(start, 4 * WORDS), :]
        for m in range(4):
            mine = words[m * WORDS : (m + 1) * WORDS]
            targets = target_ref[n * 4 + m].astype(F32)
            high = (mine[:8] >> 16, (mine[:8] << 16) >> 16)
            for half in range(halves):
                low = (jnp.broadcast_to(mine[8 + half : 9 + half], (8, 128)) >> place) & 15
                data = (high[half] * 16 + low).astype(F32)
                target = targets[half * 8 : half * 8 + 8, :]
                for t in range(8):
                    i = t * halves + half
                    acc[i] = acc[i] + jnp.where(target == float(t), data, 0.0)
        return tuple(acc)

    zero = jnp.zeros((8, 128), F32)
    acc = lax.fori_loop(0, owners // 4, step, (zero,) * (8 * halves), unroll=4)
    lane = lax.broadcasted_iota(jnp.int32, (8, 128), 1)
    even = (lane // 8) % 2 == 0
    for p in range(PD):
        for half in range(halves):
            a = acc[(2 * p) * halves + half]
            b = acc[(2 * p + 1) * halves + half]
            a = a + pltpu.roll(a, 120, 1)
            b = b + pltpu.roll(b, 8, 1)
            out_ref[pl.ds((p * halves + half) * 8, 8), :] = jnp.where(even, a, b) / (
                VIEWS * 4.0 * STEPS
            )


def column_kernel(first_ref, mid_ref, second_ref, w_ref, bias_ref, wo_ref, out_ref):
    rows = mid_ref.shape[0] // 2
    blocks = rows // PD
    x = jnp.concatenate(
        [ref[pl.ds(j * rows, rows), :] for ref in (first_ref, mid_ref, second_ref) for j in range(2)],
        axis=1,
    )
    hi = x.astype(BF16)
    rest = x - hi.astype(F32)
    mid = rest.astype(BF16)
    low = (rest - mid.astype(F32)).astype(BF16)
    y3 = jnp.dot(
        jnp.concatenate([low, mid, hi], axis=0), w_ref[...], preferred_element_type=F32
    )
    y = (y3[:rows] + y3[rows : 2 * rows]) + y3[2 * rows :]
    z = y[:, :512] + bias_ref[0:1, :]
    cand = jnp.tanh(y[:, 512:] + bias_ref[1:2, :])
    small = jnp.exp(-jnp.abs(z))
    big = 1.0 / (1.0 + small)
    small = small * big
    up = z >= 0
    retain = jnp.where(up, big, small)
    fresh = jnp.where(up, small, big) * cand
    order = [(il3, p) for il3 in range(4) for p in range(PD)]

    def cut(v, il3, p):
        return v[p * blocks : (p + 1) * blocks, il3 * 128 : (il3 + 1) * 128]

    dc = None
    for il3, p in order:
        d, o = cut(retain, il3, p), cut(fresh, il3, p)
        dc, oc = (d, o) if dc is None else (d * dc, d * oc + o)
    lane = lax.broadcasted_iota(jnp.int32, (blocks, 128), 1)
    sub = lax.broadcasted_iota(jnp.int32, (blocks, 128), 0)
    first = lane < 64
    od = pltpu.roll(dc, 64, 1)
    oo = pltpu.roll(oc, 64, 1)
    pd_all = dc * od
    po_all = jnp.where(first, od * oc + oo, dc * oo + oc)
    reach = 1
    while reach < blocks:
        sd = jnp.where(sub < reach, 1.0, pltpu.roll(pd_all, reach, 0))
        so = jnp.where(sub < reach, 0.0, pltpu.roll(po_all, reach, 0))
        po_all = pd_all * so + po_all
        pd_all = pd_all * sd
        reach *= 2
    before = jnp.where(sub < 1, 0.0, pltpu.roll(po_all, 1, 0))
    h = jnp.where(first, before, od * before + oo)
    states = {}
    for il3, p in order:
        h = cut(retain, il3, p) * h + cut(fresh, il3, p)
        states[il3, p] = h
    wide = jnp.concatenate(
        [jnp.concatenate([states[il3, p] for p in range(PD)], axis=1) for il3 in range(4)], axis=0
    )
    s = jnp.dot(wide, wo_ref[...], precision=lax.Precision.HIGHEST, preferred_element_type=F32)

    def over(op, v):
        v = jnp.broadcast_to(v, (8, 128))
        v = op(v, pltpu.roll(v, 2, 1))
        v = op(v, pltpu.roll(v, 4, 1))
        return op(v, pltpu.roll(v, 8, 1))[0:1]

    row = lax.broadcasted_iota(jnp.int32, (rows, 128), 0)
    col = lax.broadcasted_iota(jnp.int32, (rows, 128), 1)
    plane = (row % blocks) * 32 + ((col // 8) % 2) * 16 + (row // blocks) * 4 + (col % 8) // 2
    value = 1.0 / (0.1 + 0.9 * plane.astype(F32) / (PD * 8 * blocks - 1))
    highest = over(jnp.maximum, jnp.max(s, axis=0, keepdims=True))
    weights = jnp.exp(s - highest)
    total = over(jnp.add, jnp.sum(weights, axis=0, keepdims=True))
    depth = over(jnp.add, jnp.sum(weights * value, axis=0, keepdims=True))
    prob = weights / total
    expected = depth / total
    for u in range(2):
        mine = prob if u == 0 else pltpu.roll(prob, 120, 1)
        message = jnp.where(col < 8, mine, expected)
        for il3 in range(4):
            out_ref[pl.ds(u * 4 + il3, blocks, stride=8), :] = message[
                il3 * blocks : (il3 + 1) * blocks
            ]


def output_kernel(x_ref, prob_ref, map_ref, ordered):
    for column, k in enumerate(path()):
        ordered[column : column + 1, :] = x_ref[k : k + 1, :]
    t = ordered[...].T
    for p in range(PD):
        prob_ref[p] = t[p * 2 : p * 2 + 2]
    map_ref[...] = t[8:10]


def gate_rows(w_gates, slab, odd):
    w = w_gates.reshape(3, 3, 2, 32, 8).transpose(0, 1, 4, 2, 3)
    w = jnp.pad(w, ((2, 2), (0, 0), (0, 0), (0, 0), (0, 0)))
    by_row = [lax.dynamic_slice_in_dim(w, 3 - r - 2 * slab, 4, axis=0) for r in range(2)]
    v = jnp.stack(by_row, axis=4).reshape(2, 2, 3, 8, 2, 2, 32)
    v = jnp.where(odd, v[:, :, ::-1], v)
    v = v.transpose(4, 2, 0, 1, 3, 5, 6).reshape(2, 96, 64)
    return jnp.concatenate([v, v], axis=2)


def body(ref_feat, src_feat, tile_owner, tile_local, col_shift, w_gates, bias_z, bias_c, w_out):
    owners = lax.axis_size("depth")
    row_count, feat, cols = ref_feat.shape
    requests = tile_local.shape[0]
    tiles = src_feat.shape[0]
    blocks = owners // 8
    message = pl.pallas_call(
        message_kernel,
        out_shape=jax.ShapeDtypeStruct((owners, 128), jnp.int32),
        in_specs=[pl.BlockSpec(memory_space=pltpu.HBM)] * 3,
        out_specs=vspec(),
        scratch_shapes=[pltpu.VMEM((1, requests), jnp.int32)] * 3 + [pltpu.SemaphoreType.DMA((3,))],
        compiler_params=params(60),
        name="message",
    )(*[v.reshape(1, requests) for v in (tile_owner, tile_local, col_shift)])
    message = message.reshape(owners, 1, 128)
    asked = lax.all_to_all(message, "depth", split_axis=0, concat_axis=0, tiled=True)
    asked = asked.reshape(owners, 128)

    table, channels = pl.pallas_call(
        prepare_kernel,
        out_shape=(
            jax.ShapeDtypeStruct((row_count * (2 * MAXSHIFT + 1), feat, cols), F32),
            jax.ShapeDtypeStruct((tiles, feat, cols), BF16),
        ),
        in_specs=[vspec(), vspec()],
        out_specs=(vspec(), vspec()),
        scratch_shapes=[
            pltpu.VMEM((row_count * feat, cols), F32),
            pltpu.VMEM((tiles * feat, cols), F32),
        ],
        compiler_params=params(16),
        cost_estimate=pl.CostEstimate(flops=2000000, transcendentals=0, bytes_accessed=4000000),
        name="prepare",
    )(ref_feat, src_feat)

    def answers_of(*refs):
        answer_kernel(requests, *refs)

    answers = pl.pallas_call(
        answers_of,
        out_shape=jax.ShapeDtypeStruct((cols * WORDS, 128), jnp.int32),
        in_specs=[vspec(), vspec(), vspec()],
        out_specs=pl.BlockSpec(memory_space=pl.ANY),
        scratch_shapes=[
            pltpu.VMEM((cols * blocks, 128), F32),
            pltpu.VMEM((cols * WORDS, 128), jnp.int32),
            pltpu.VMEM((8, owners), jnp.int32),
            pltpu.SMEM((8, owners), jnp.int32),
            pltpu.SemaphoreType.DMA,
            pltpu.SemaphoreType.DMA((PIECES,)),
        ],
        compiler_params=params(10),
        name="answer",
    )(asked, table, channels)
    answers = lax.all_to_all(
        answers.reshape(cols, 1, WORDS * 128), "depth", split_axis=0, concat_axis=0, tiled=True
    )

    slab = lax.axis_index("slab")
    depth = lax.axis_index("depth")
    odd = (depth // (TORUS[1] * TORUS[2]) + depth // TORUS[2] + depth) % 2 == 1

    def tables_of(*refs):
        table_kernel(requests, *refs)

    targets, gates = pl.pallas_call(
        tables_of,
        out_shape=(
            jax.ShapeDtypeStruct((owners, blocks, 128), BF16),
            jax.ShapeDtypeStruct((768, 1024), BF16),
        ),
        in_specs=[vspec(), vspec()],
        out_specs=(vspec(), vspec()),
        scratch_shapes=[pltpu.VMEM((requests * blocks, 128), F32)],
        compiler_params=params(8),
        cost_estimate=pl.CostEstimate(flops=20000000, transcendentals=0, bytes_accessed=3000000),
        name="tables",
    )(asked, gate_rows(w_gates, slab, odd))

    cost = pl.pallas_call(
        combine_kernel,
        out_shape=jax.ShapeDtypeStruct((PD * blocks, 128), F32),
        in_specs=[vspec(), vspec()],
        out_specs=vspec(),
        compiler_params=params(6),
        name="combine",
    )(answers.reshape(owners * WORDS, 128), targets)
    both = lax.all_gather(cost, "slab", tiled=True)
    chips = path()

    def exchange(start):
        pairs = [(chips[i], chips[i + 1]) for i in range(start, owners - 1, 2)]
        return lax.ppermute(both, "depth", pairs + [(b, a) for a, b in pairs])

    first, second = exchange(1), exchange(0)

    bias = jnp.stack([jnp.tile(bias_z, 16), jnp.tile(bias_c, 16)])
    unit_row = jnp.arange(512, dtype=jnp.int32)[:, None] // 32
    unit_row = ((unit_row // 2) % 2) * 8 + (unit_row // 4) * 2 + unit_row % 2
    score_col = jnp.arange(128, dtype=jnp.int32)[None, :] % 16
    project = jnp.where(unit_row == score_col, jnp.tile(w_out, 16)[:, None], 0.0)
    packed = pl.pallas_call(
        column_kernel,
        out_shape=jax.ShapeDtypeStruct((owners, 128), F32),
        in_specs=[vspec()] * 6,
        out_specs=vspec(),
        compiler_params=params(10),
        name="column",
    )(first, both, second, gates, bias, project)
    packed = lax.all_to_all(
        packed.reshape(owners, 1, 128), "depth", split_axis=0, concat_axis=0, tiled=True
    )
    return pl.pallas_call(
        output_kernel,
        out_shape=(
            jax.ShapeDtypeStruct((PD, row_count, cols), F32),
            jax.ShapeDtypeStruct((row_count, cols), F32),
        ),
        in_specs=[vspec()],
        out_specs=(vspec(), vspec()),
        scratch_shapes=[pltpu.VMEM((cols, 128), F32)],
        compiler_params=params(4),
        name="output",
    )(packed.reshape(cols, 128))


def solution(mesh):
    return jax.shard_map(
        body,
        mesh=mesh,
        in_specs=(
            P("slab", None, None),
            P("depth", None, None),
            P(("depth", "slab"), None),
            P(("depth", "slab")),
            P(("depth", "slab")),
            P(),
            P(),
            P(),
            P(),
        ),
        out_specs=(P("depth", "slab", None), P("slab", None)),
        check_vma=False,
    )
```

```python
import jax
import jax.numpy as jnp
from jax import lax
from jax.experimental import pallas as pl
from jax.experimental.pallas import tpu as pltpu
from jax.sharding import PartitionSpec as P

VIEWS = 5
STEPS = 1618.0
PD = 4
MAXSHIFT = 16
F32 = jnp.float32
BF16 = jnp.bfloat16
UNROLL = 16
PIECES = 8
WORDS = 10
MIB = 1024 * 1024
TORUS = (4, 4, 8)


def params(mib):
    return pltpu.CompilerParams(vmem_limit_bytes=mib * MIB)


def column_of(k):
    nx, ny, nz = TORUS
    x, y, z = k // (ny * nz), (k // nz) % ny, k % nz
    place = x * ny + (ny - 1 - y if x % 2 else y)
    return z * nx * ny + (nx * ny - 1 - place if z % 2 else place)


def path():
    return sorted(range(TORUS[0] * TORUS[1] * TORUS[2]), key=column_of)


def message_kernel(a_ref, b_ref, c_ref, out_ref, a_s, b_s, c_s, sems):
    copies = [
        pltpu.make_async_copy(ref, scratch, sems.at[n])
        for n, (ref, scratch) in enumerate(((a_ref, a_s), (b_ref, b_s), (c_ref, c_s)))
    ]
    for copy in copies:
        copy.start()
    for copy in copies:
        copy.wait()
    rest = jnp.zeros((1, 128 - 3 * a_s.shape[1]), jnp.int32)
    row = jnp.concatenate([a_s[...], b_s[...], c_s[...], rest], axis=1)
    out_ref[...] = jnp.broadcast_to(row, out_ref.shape)


def vspec():
    return pl.BlockSpec(memory_space=pltpu.VMEM)


def sspec():
    return pl.BlockSpec(memory_space=pltpu.SMEM)


def prepare_kernel(ref_ref, src_ref, tab_ref, srce_ref, ref32, src32):
    rows, feat, cols = ref_ref.shape
    tiles = src_ref.shape[0]
    cpg = feat // 8
    for r in range(rows):
        ref32[pl.ds(r * feat, feat), :] = ref_ref[r].astype(F32)
    lane = lax.broadcasted_iota(jnp.int32, (8, cols), 1)
    for r in range(rows):
        for e in range(cpg):
            base = ref32[pl.ds(r * feat + e, 8, stride=cpg), :]
            for k in range(2 * MAXSHIFT + 1):
                shift = k - MAXSHIFT
                moved = base if shift == 0 else pltpu.roll(base, (-shift) % cols, 1)
                inside = (lane + shift >= 0) & (lane + shift < cols)
                tab_ref[r * (2 * MAXSHIFT + 1) + k, pl.ds(e * 8, 8), :] = jnp.where(inside, moved, 0.0)

    def widen(n, c):
        src32[pl.ds(n * feat, feat), :] = src_ref[n].astype(F32)
        return c

    lax.fori_loop(0, tiles, widen, 0, unroll=8)

    def reorder(n, c):
        parts = [src32[pl.ds(n * feat + e, 8, stride=cpg), :] for e in range(cpg)]
        srce_ref[n] = jnp.concatenate(parts, axis=0).astype(BF16)
        return c

    lax.fori_loop(0, tiles, reorder, 0, unroll=8)


def answer_kernel(requests, req_ref, tab_ref, srce_ref, out_ref, flat_s, coded_s, codes, table, sem, out_sem):
    owners = req_ref.shape[0]
    cols = tab_ref.shape[-1]
    blocks = owners // 8
    me = lax.axis_index("depth")
    flat = req_ref[...].T
    owner = flat[0:requests]
    local = flat[requests : 2 * requests]
    shift = flat[2 * requests : 3 * requests]
    q = lax.broadcasted_iota(jnp.int32, (requests, owners), 0)
    hit = owner == me
    first = jnp.min(jnp.where(hit, q, requests), axis=0, keepdims=True)
    last = jnp.max(jnp.where(hit, q, -1), axis=0, keepdims=True)
    value = local + (shift + MAXSHIFT) * 256 + (q % 2) * 16384
    zero = jnp.zeros_like(value)
    code0 = jnp.sum(jnp.where(hit & (q == first), value, zero), axis=0, keepdims=True)
    code1 = jnp.sum(jnp.where(hit & (q == last) & (q > first), value, zero), axis=0, keepdims=True)
    sub = lax.broadcasted_iota(jnp.int32, (8, owners), 0)
    codes[...] = jnp.where(sub == 0, code0, jnp.where(sub == 1, code1, 0))
    copy = pltpu.make_async_copy(codes, table, sem)
    copy.start()
    copy.wait()

    def one(i, s):
        code = table[s, i]
        loc = code & 255
        moved = (code >> 8) & 63
        row = code >> 14
        tile = srce_ref[loc].astype(F32) * tab_ref[row * (2 * MAXSHIFT + 1) + moved]
        total = (tile[0:8] + tile[8:16]) + (tile[16:24] + tile[24:32])
        return pltpu.roll(total, (moved + cols - MAXSHIFT) % cols, 1)

    def step(b, c):
        parts = []
        for il in range(8):
            for s in range(2):
                parts.append(one(b * 8 + il, s))
        flat_s[pl.ds(b, cols, stride=blocks), :] = jnp.concatenate(parts, axis=0).T
        return c

    lax.fori_loop(0, blocks, step, 0, unroll=UNROLL)

    half = blocks // 2
    place = lax.broadcasted_iota(jnp.int32, (half, cols), 0) * 4
    size = cols // PIECES
    copies = []
    for n in range(PIECES):
        for k in range(n * size, (n + 1) * size):
            start = column_of(k) * blocks
            number = jnp.round(flat_s[start : start + blocks, :] * STEPS).astype(jnp.int32)
            high = number >> 4
            low = number & 15
            at = k * WORDS
            coded_s[at : at + half, :] = (high[:half] << 16) | (high[half:] & 65535)
            coded_s[at + half : at + half + 1, :] = jnp.sum(
                low[:half] << place, axis=0, keepdims=True
            )
            coded_s[at + half + 1 : at + WORDS, :] = jnp.sum(
                low[half:] << place, axis=0, keepdims=True
            )
        piece = pl.ds(n * size * WORDS, size * WORDS)
        copies.append(pltpu.make_async_copy(coded_s.at[piece], out_ref.at[piece], out_sem.at[n]))
        copies[-1].start()
    for copy in copies:
        copy.wait()


def table_kernel(requests, req_ref, wd_ref, target_ref, gate_ref, keys):
    owners = req_ref.shape[0]
    blocks = owners // 8
    flat = req_ref[...].T
    owner = flat[0:requests]
    q = lax.broadcasted_iota(jnp.int32, (requests, owners), 0)
    earlier = jnp.zeros((requests, owners), jnp.int32)
    for other in range(requests - 1):
        same = (owner == owner[other : other + 1]) & (q > other)
        earlier = jnp.where(same, 1, earlier)
    key = (owner * 2 + earlier).astype(F32)
    block_row = lax.broadcasted_iota(jnp.int32, (blocks, owners), 0)
    block_of = lax.broadcasted_iota(jnp.int32, (blocks, owners), 1) // 8
    own_block = block_row == block_of
    spread = []
    for n in range(requests):
        row = jnp.broadcast_to(key[n : n + 1], (blocks, owners))
        spread.append(jnp.where(own_block, row, 0.0).astype(BF16))
    inner = lax.broadcasted_iota(jnp.int32, (owners, 128), 0) % 8
    lane = lax.broadcasted_iota(jnp.int32, (owners, 128), 1)
    pick = jnp.where(inner == lane // 16, 1.0, 0.0).astype(BF16)
    wide = jnp.dot(jnp.concatenate(spread, axis=0), pick, preferred_element_type=F32)
    slot = (lax.broadcasted_iota(jnp.int32, (blocks * requests, 128), 1) // 8) % 2
    keys[...] = wide - slot.astype(F32)

    def step(n, c):
        found = [[jnp.full((8, 128), 8.0, F32) for _ in range(blocks // 8)] for _ in range(4)]
        wanted = [(2 * (n * 4 + m)).astype(F32) for m in range(4)]
        for r in range(requests):
            t = float((r // (2 * VIEWS)) * 2 + r % 2)
            for half in range(blocks // 8):
                k = keys[r * blocks + half * 8 : r * blocks + half * 8 + 8, :]
                for m in range(4):
                    found[m][half] = jnp.where(k == wanted[m], t, found[m][half])
        for m in range(4):
            target_ref[n * 4 + m] = jnp.concatenate(found[m], axis=0).astype(BF16)
        return c

    lax.fori_loop(0, owners // 4, step, 0)

    half_of = lax.broadcasted_iota(jnp.int32, (16, 128), 1) // 64
    for source in range(6):
        for zc in range(2):
            part = wd_ref[zc, source * 16 : source * 16 + 16, :]
            for il in range(8):
                mine = jnp.where(half_of == il // 4, part, jnp.zeros_like(part))
                for il3 in range(4):
                    value = mine if il3 == il % 4 else jnp.zeros_like(part)
                    gate_ref[
                        pl.ds(source * 128 + il * 16, 16), pl.ds((zc * 4 + il3) * 128, 128)
                    ] = value


def combine_kernel(ans_ref, target_ref, out_ref):
    owners = target_ref.shape[0]
    halves = target_ref.shape[1] // 8
    place = lax.broadcasted_iota(jnp.int32, (8, 128), 0) * 4

    def step(n, acc):
        acc = list(acc)
        start = pl.multiple_of(n * 4 * WORDS, 8)
        words = ans_ref[pl.ds(start, 4 * WORDS), :]
        for m in range(4):
            mine = words[m * WORDS : (m + 1) * WORDS]
            targets = target_ref[n * 4 + m].astype(F32)
            high = (mine[:8] >> 16, (mine[:8] << 16) >> 16)
            for half in range(halves):
                low = (jnp.broadcast_to(mine[8 + half : 9 + half], (8, 128)) >> place) & 15
                data = (high[half] * 16 + low).astype(F32)
                target = targets[half * 8 : half * 8 + 8, :]
                for t in range(8):
                    i = t * halves + half
                    acc[i] = acc[i] + jnp.where(target == float(t), data, 0.0)
        return tuple(acc)

    zero = jnp.zeros((8, 128), F32)
    acc = lax.fori_loop(0, owners // 4, step, (zero,) * (8 * halves), unroll=4)
    lane = lax.broadcasted_iota(jnp.int32, (8, 128), 1)
    even = (lane // 8) % 2 == 0
    for p in range(PD):
        for half in range(halves):
            a = acc[(2 * p) * halves + half]
            b = acc[(2 * p + 1) * halves + half]
            a = a + pltpu.roll(a, 120, 1)
            b = b + pltpu.roll(b, 8, 1)
            out_ref[pl.ds((p * halves + half) * 8, 8), :] = jnp.where(even, a, b) / (
                VIEWS * 4.0 * STEPS
            )


def column_kernel(first_ref, mid_ref, second_ref, w_ref, bias_ref, wo_ref, out_ref):
    rows = mid_ref.shape[0] // 2
    blocks = rows // PD
    x = jnp.concatenate(
        [ref[pl.ds(j * rows, rows), :] for ref in (first_ref, mid_ref, second_ref) for j in range(2)],
        axis=1,
    )
    hi = x.astype(BF16)
    rest = x - hi.astype(F32)
    mid = rest.astype(BF16)
    low = (rest - mid.astype(F32)).astype(BF16)
    y3 = jnp.dot(
        jnp.concatenate([low, mid, hi], axis=0), w_ref[...], preferred_element_type=F32
    )
    y = (y3[:rows] + y3[rows : 2 * rows]) + y3[2 * rows :]
    z = y[:, :512] + bias_ref[0:1, :]
    cand = jnp.tanh(y[:, 512:] + bias_ref[1:2, :])
    small = jnp.exp(-jnp.abs(z))
    big = 1.0 / (1.0 + small)
    small = small * big
    up = z >= 0
    retain = jnp.where(up, big, small)
    fresh = jnp.where(up, small, big) * cand
    order = [(il3, p) for il3 in range(4) for p in range(PD)]

    def cut(v, il3, p):
        return v[p * blocks : (p + 1) * blocks, il3 * 128 : (il3 + 1) * 128]

    dc = None
    for il3, p in order:
        d, o = cut(retain, il3, p), cut(fresh, il3, p)
        dc, oc = (d, o) if dc is None else (d * dc, d * oc + o)
    lane = lax.broadcasted_iota(jnp.int32, (blocks, 128), 1)
    sub = lax.broadcasted_iota(jnp.int32, (blocks, 128), 0)
    first = lane < 64
    od = pltpu.roll(dc, 64, 1)
    oo = pltpu.roll(oc, 64, 1)
    pd_all = dc * od
    po_all = jnp.where(first, od * oc + oo, dc * oo + oc)
    reach = 1
    while reach < blocks:
        sd = jnp.where(sub < reach, 1.0, pltpu.roll(pd_all, reach, 0))
        so = jnp.where(sub < reach, 0.0, pltpu.roll(po_all, reach, 0))
        po_all = pd_all * so + po_all
        pd_all = pd_all * sd
        reach *= 2
    before = jnp.where(sub < 1, 0.0, pltpu.roll(po_all, 1, 0))
    h = jnp.where(first, before, od * before + oo)
    states = {}
    for il3, p in order:
        h = cut(retain, il3, p) * h + cut(fresh, il3, p)
        states[il3, p] = h
    wide = jnp.concatenate(
        [jnp.concatenate([states[il3, p] for p in range(PD)], axis=1) for il3 in range(4)], axis=0
    )
    s = jnp.dot(wide, wo_ref[...], precision=lax.Precision.HIGHEST, preferred_element_type=F32)

    def over(op, v):
        v = jnp.broadcast_to(v, (8, 128))
        v = op(v, pltpu.roll(v, 2, 1))
        v = op(v, pltpu.roll(v, 4, 1))
        return op(v, pltpu.roll(v, 8, 1))[0:1]

    row = lax.broadcasted_iota(jnp.int32, (rows, 128), 0)
    col = lax.broadcasted_iota(jnp.int32, (rows, 128), 1)
    plane = (row % blocks) * 32 + ((col // 8) % 2) * 16 + (row // blocks) * 4 + (col % 8) // 2
    value = 1.0 / (0.1 + 0.9 * plane.astype(F32) / (PD * 8 * blocks - 1))
    highest = over(jnp.maximum, jnp.max(s, axis=0, keepdims=True))
    weights = jnp.exp(s - highest)
    total = over(jnp.add, jnp.sum(weights, axis=0, keepdims=True))
    depth = over(jnp.add, jnp.sum(weights * value, axis=0, keepdims=True))
    prob = weights / total
    expected = depth / total
    for u in range(2):
        mine = prob if u == 0 else pltpu.roll(prob, 120, 1)
        message = jnp.where(col < 8, mine, expected)
        for il3 in range(4):
            out_ref[pl.ds(u * 4 + il3, blocks, stride=8), :] = message[
                il3 * blocks : (il3 + 1) * blocks
            ]


def output_kernel(x_ref, prob_ref, map_ref, ordered):
    for column, k in enumerate(path()):
        ordered[column : column + 1, :] = x_ref[k : k + 1, :]
    t = ordered[...].T
    for p in range(PD):
        prob_ref[p] = t[p * 2 : p * 2 + 2]
    map_ref[...] = t[8:10]


def gate_rows(w_gates, slab, turned):
    w = w_gates.reshape(3, 3, 2, 32, 8).transpose(0, 1, 4, 2, 3)
    w = jnp.pad(w, ((2, 2), (0, 0), (0, 0), (0, 0), (0, 0)))
    by_row = [lax.dynamic_slice_in_dim(w, 3 - r - 2 * slab, 4, axis=0) for r in range(2)]
    v = jnp.stack(by_row, axis=4).reshape(2, 2, 3, 8, 2, 2, 32)
    v = jnp.where(turned, v[:, :, ::-1], v)
    v = v.transpose(4, 2, 0, 1, 3, 5, 6).reshape(2, 96, 64)
    return jnp.concatenate([v, v], axis=2)


def body(ref_feat, src_feat, tile_owner, tile_local, col_shift, w_gates, bias_z, bias_c, w_out):
    owners = lax.axis_size("depth")
    row_count, feat, cols = ref_feat.shape
    requests = tile_local.shape[0]
    tiles = src_feat.shape[0]
    blocks = owners // 8
    message = pl.pallas_call(
        message_kernel,
        out_shape=jax.ShapeDtypeStruct((owners, 128), jnp.int32),
        in_specs=[pl.BlockSpec(memory_space=pltpu.HBM)] * 3,
        out_specs=vspec(),
        scratch_shapes=[pltpu.VMEM((1, requests), jnp.int32)] * 3 + [pltpu.SemaphoreType.DMA((3,))],
        compiler_params=params(60),
        name="message",
    )(*[v.reshape(1, requests) for v in (tile_owner, tile_local, col_shift)])
    message = message.reshape(owners, 1, 128)
    asked = lax.all_to_all(message, "depth", split_axis=0, concat_axis=0, tiled=True)
    asked = asked.reshape(owners, 128)

    table, channels = pl.pallas_call(
        prepare_kernel,
        out_shape=(
            jax.ShapeDtypeStruct((row_count * (2 * MAXSHIFT + 1), feat, cols), F32),
            jax.ShapeDtypeStruct((tiles, feat, cols), BF16),
        ),
        in_specs=[vspec(), vspec()],
        out_specs=(vspec(), vspec()),
        scratch_shapes=[
            pltpu.VMEM((row_count * feat, cols), F32),
            pltpu.VMEM((tiles * feat, cols), F32),
        ],
        compiler_params=params(16),
        cost_estimate=pl.CostEstimate(flops=2000000, transcendentals=0, bytes_accessed=4000000),
        name="prepare",
    )(ref_feat, src_feat)

    def answers_of(*refs):
        answer_kernel(requests, *refs)

    answers = pl.pallas_call(
        answers_of,
        out_shape=jax.ShapeDtypeStruct((cols * WORDS, 128), jnp.int32),
        in_specs=[vspec(), vspec(), vspec()],
        out_specs=pl.BlockSpec(memory_space=pl.ANY),
        scratch_shapes=[
            pltpu.VMEM((cols * blocks, 128), F32),
            pltpu.VMEM((cols * WORDS, 128), jnp.int32),
            pltpu.VMEM((8, owners), jnp.int32),
            pltpu.SMEM((8, owners), jnp.int32),
            pltpu.SemaphoreType.DMA,
            pltpu.SemaphoreType.DMA((PIECES,)),
        ],
        compiler_params=params(10),
        name="answer",
    )(asked, table, channels)
    answers = lax.all_to_all(
        answers.reshape(cols, 1, WORDS * 128), "depth", split_axis=0, concat_axis=0, tiled=True
    )

    slab = lax.axis_index("slab")
    depth = lax.axis_index("depth")
    even = (depth // (TORUS[1] * TORUS[2]) + depth // TORUS[2] + depth) % 2 == 0

    def tables_of(*refs):
        table_kernel(requests, *refs)

    targets, gates = pl.pallas_call(
        tables_of,
        out_shape=(
            jax.ShapeDtypeStruct((owners, blocks, 128), BF16),
            jax.ShapeDtypeStruct((768, 1024), BF16),
        ),
        in_specs=[vspec(), vspec()],
        out_specs=(vspec(), vspec()),
        scratch_shapes=[pltpu.VMEM((requests * blocks, 128), F32)],
        compiler_params=params(8),
        cost_estimate=pl.CostEstimate(flops=20000000, transcendentals=0, bytes_accessed=3000000),
        name="tables",
    )(asked, gate_rows(w_gates, slab, even))

    cost = pl.pallas_call(
        combine_kernel,
        out_shape=jax.ShapeDtypeStruct((PD * blocks, 128), F32),
        in_specs=[vspec(), vspec()],
        out_specs=vspec(),
        compiler_params=params(6),
        name="combine",
    )(answers.reshape(owners * WORDS, 128), targets)
    both = lax.all_gather(cost, "slab", tiled=True)
    chips = path()

    def exchange(start):
        pairs = [(chips[i], chips[i + 1]) for i in range(start, owners - 1, 2)]
        return lax.ppermute(both, "depth", pairs + [(b, a) for a, b in pairs])

    first, second = exchange(0), exchange(1)

    bias = jnp.stack([jnp.tile(bias_z, 16), jnp.tile(bias_c, 16)])
    unit_row = jnp.arange(512, dtype=jnp.int32)[:, None] // 32
    unit_row = ((unit_row // 2) % 2) * 8 + (unit_row // 4) * 2 + unit_row % 2
    score_col = jnp.arange(128, dtype=jnp.int32)[None, :] % 16
    project = jnp.where(unit_row == score_col, jnp.tile(w_out, 16)[:, None], 0.0)
    packed = pl.pallas_call(
        column_kernel,
        out_shape=jax.ShapeDtypeStruct((owners, 128), F32),
        in_specs=[vspec()] * 6,
        out_specs=vspec(),
        compiler_params=params(10),
        name="column",
    )(first, both, second, gates, bias, project)
    packed = lax.all_to_all(
        packed.reshape(owners, 1, 128), "depth", split_axis=0, concat_axis=0, tiled=True
    )
    return pl.pallas_call(
        output_kernel,
        out_shape=(
            jax.ShapeDtypeStruct((PD, row_count, cols), F32),
            jax.ShapeDtypeStruct((row_count, cols), F32),
        ),
        in_specs=[vspec()],
        out_specs=(vspec(), vspec()),
        scratch_shapes=[pltpu.VMEM((cols, 128), F32)],
        compiler_params=params(4),
        name="output",
    )(packed.reshape(cols, 128))


def solution(mesh):
    return jax.shard_map(
        body,
        mesh=mesh,
        in_specs=(
            P("slab", None, None),
            P("depth", None, None),
            P(("depth", "slab"), None),
            P(("depth", "slab")),
            P(("depth", "slab")),
            P(),
            P(),
            P(),
            P(),
        ),
        out_specs=(P("depth", "slab", None), P("slab", None)),
        check_vma=False,
    )
```
